512 devices in a mesh: dp: 32 (over y, x), seq: 16 (over z, core).
Axes of the slice: x: 4, y: 8, z: 8, core: 2. Of those that a mesh axis runs over, the one named last changes fastest.
Arguments:
- ssm_input: bfloat16 [32, 2048, 1024], P('dp', 'seq'), may hold values from -3 to 3
- state_in: bfloat16 [32, 2048, 128], P('dp', 'seq'), may hold values from -0.59765625 to 0.59765625
- state_out: bfloat16 [32, 2048, 128], P('dp', 'seq'), may hold values from -0.59765625 to 0.59765625
- step_size: float32 [32, 8, 2048], P('dp', None, 'seq'), may hold values from 0.5 to 2
- decay_rate: float32 [8], replicated, may hold values from 0.00012207031 to 0.03
- view_keep: float32 [8], replicated, may hold values from 0.6 to 0.9
- skip_gain: float32 [8], replicated, may hold values from 0.5 to 1.5
- view_lengths: int32 [32, 8], P('dp'), may hold values from 1 to 512, 2048 in all within a row
- queries: bfloat16 [32, 2048, 512], P('dp', 'seq'), may hold values from -140 to 140
- key_vectors: bfloat16 [32, 2048, 512], P('dp', 'seq'), may hold values from -5 to 5
- covisible: int32 [32, 16, 4], P('dp'), may hold values from 0 to 15, as said below
- grad_out: bfloat16 [32, 2048, 1024], P('dp', 'seq'), may hold values from -6 to 6
Outputs:
- attended: bfloat16 [32, 2048, 1024], P('dp', 'seq')
- grad_queries: bfloat16 [32, 2048, 512], P('dp', 'seq')
- grad_keys: bfloat16 [32, 2048, 512], P('dp', 'seq')
- grad_input: bfloat16 [32, 2048, 1024], P('dp', 'seq')
- grad_state_in: bfloat16 [32, 2048, 128], P('dp', 'seq')
- grad_state_out: bfloat16 [32, 2048, 128], P('dp', 'seq')
- grad_step: float32 [32, 8, 2048], P('dp', None, 'seq')
- grad_rate: float32 [8], replicated
- grad_keep: float32 [8], replicated
- grad_skip: float32 [8], replicated
The draws below stay inside these ranges and needn't reach their ends.
Inputs may be any that keep to these rules, and one draw needn't show every extreme that they name: `view_lengths`: the 8 lengths of a scene sum to 2048; the largest is exactly 512. `covisible`: each row names 4 different blocks of the scene; the first is the row's own block.
All inputs are finite; a program needn't handle non-finite values.
Results may differ from the reference program's by a relative error of at most 0.007.
Values may be sent and summed in bfloat16 or wider, within the bound.
A program may use at most 64 MiB of HBM per device.

```python
import math
from functools import partial
import jax
import jax.numpy as jnp
import numpy as np
from jax import lax

TOK_DEV = 128
BLK = 128
HEADS = 8
HEAD = 128
STATE = 128
QK = 64
LISTED = 4
VIEWS = 8
SCENES = 32
TOKENS = 2048
NBLK = 16
N_SEQ = 16


def pair_rows(key):
    base_key = jax.random.fold_in(key, 7001)
    full_shape = (SCENES, TOKENS, HEADS * QK)
    query_draw = jnp.clip(jax.random.normal(jax.random.fold_in(base_key, 1), full_shape, jnp.float32), -5.0, 5.0)
    key_draw = jnp.clip(jax.random.normal(jax.random.fold_in(base_key, 2), full_shape, jnp.float32), -5.0, 5.0)
    return (query_draw, key_draw)


def draw_queries(key, part):
    return pair_rows(key)[0].astype(jnp.bfloat16)


def draw_key_vectors(key, part):
    return pair_rows(key)[1].astype(jnp.bfloat16)


def draw_covisible(key, part):
    base_key = jax.random.fold_in(key, 7002)
    popular = jax.random.randint(jax.random.fold_in(base_key, 1), (SCENES, 1, NBLK), 0, 2048)
    jitter_draw = jax.random.randint(jax.random.fold_in(base_key, 2), (SCENES, NBLK, NBLK), 0, 4096)
    columns = jnp.arange(NBLK, dtype=jnp.int32)
    ranking = (jitter_draw + popular) * NBLK + columns[None, None, :]
    ranking = jnp.where((columns[:, None] == columns[None, :])[None], 2 ** 30, ranking)
    chosen = lax.top_k(ranking, LISTED)[1]
    return chosen.astype(jnp.int32)


def levels(stream_key, dims, pieces, low, largest):
    level = 1.0
    for dim, shards_of in pieces:
        steps = jax.random.uniform(jax.random.fold_in(jax.random.fold_in(stream_key, 6), dim), (shards_of,), jnp.float32, low / len(pieces), largest / len(pieces))
        level = level * jnp.repeat(jnp.exp(steps), dims[dim] // shards_of).reshape((-1,) + (1,) * (len(dims) - 1 - dim))
    return level


def split_up(count, total, limit, skew):
    loads = [(1 << 20) // math.isqrt(standing ** skew) + 1 for standing in range(2, count + 1)]
    rest, counts = total - limit - (count - 1), [1] * (count - 1)
    while rest > 0:
        movable = [i for i in range(count - 1) if counts[i] < limit]
        pool, left = sum([loads[i] for i in movable]), rest
        for i in movable:
            addition = min(limit - counts[i], max(1, left * loads[i] // pool), rest)
            counts[i] = counts[i] + addition
            rest = rest - addition
    return np.array([limit] + counts)


def ragged(own_key, amount, total, bound, slope):
    if amount == 2:
        one = jax.random.randint(own_key, (), max(1, total - bound), min(bound, total - 1) + 1)
        return jnp.stack([one, total - one])
    lengths = jnp.asarray(split_up(amount, total, bound, slope), jnp.int32)
    twos = (amount - 1) // 2
    source_of, taker = lengths[1:1 + 2 * twos:2], lengths[2:2 + 2 * twos:2]
    margin = jnp.minimum(source_of - 1, bound - taker)
    shifted = jax.random.randint(jax.random.fold_in(own_key, 1), (twos,), 0, 1 << 20) % (margin + 1)
    lengths = lengths.at[1:1 + 2 * twos:2].set(source_of - shifted).at[2:2 + 2 * twos:2].set(taker + shifted)
    return lengths[jax.random.permutation(jax.random.fold_in(own_key, 2), amount)]


def scatter_about(rng, shape, spread, bound, pieces=(), held_as=jnp.bfloat16):
    gain = levels(rng, shape, pieces, -0.22, 0.18) if pieces else 1.0
    values = jax.random.normal(rng, shape, jnp.float32) * spread * gain
    return jnp.minimum(jnp.maximum(values, -bound), bound).astype(held_as)


def setup_inputs(seed: int = 0) -> dict:
    keys = jax.random.split(jax.random.key(seed), 13)
    ssm_input = scatter_about(keys[0], (SCENES, TOKENS, HEADS * HEAD), 0.5, 3.0, ((0, 32), (1, 16)))
    state_in = scatter_about(keys[1], (SCENES, TOKENS, STATE), 0.1, 0.59765625, ((0, 32), (1, 16)))
    state_out = scatter_about(keys[2], (SCENES, TOKENS, STATE), 0.1, 0.59765625, ((0, 32), (1, 16)))
    step_size = jnp.clip(jnp.exp(math.log(2.0) - 1.3862944 * jax.random.uniform(keys[3], (SCENES, HEADS, TOKENS), jnp.float32) ** levels(keys[3], (SCENES, HEADS, TOKENS), ((0, 32), (2, 16)), -0.2, 0.2)), 0.5, 2.0)
    decay_rate = jnp.clip(jnp.exp(jax.random.uniform(keys[4], (HEADS,), jnp.float32, math.log(0.00012207031), math.log(0.03))), 0.00012207031, 0.03)
    view_keep = jnp.clip(jax.random.uniform(keys[5], (HEADS,), jnp.float32, 0.6, 0.9), 0.6, 0.9)
    skip_gain = jnp.clip(jax.random.uniform(keys[6], (HEADS,), jnp.float32, 0.5, 1.5), 0.5, 1.5)
    view_lengths = jax.vmap(lambda own: ragged(own, VIEWS, TOKENS, TOKENS // 4, 2))(jax.random.split(keys[7], SCENES)).reshape((SCENES, VIEWS)).astype(jnp.int32)
    queries = draw_queries(jax.random.fold_in(keys[12], 71), 0)
    key_vectors = draw_key_vectors(jax.random.fold_in(keys[12], 71), 0)
    covisible = draw_covisible(jax.random.fold_in(keys[12], 71), 0)
    grad_out = scatter_about(keys[11], (SCENES, TOKENS, HEADS * HEAD), 1.0, 6.0, ((0, 32), (1, 16)))
    return {"ssm_input": ssm_input, "state_in": state_in, "state_out": state_out, "step_size": step_size, "decay_rate": decay_rate, "view_keep": view_keep, "skip_gain": skip_gain, "view_lengths": view_lengths, "queries": queries, "key_vectors": key_vectors, "covisible": covisible, "grad_out": grad_out}


HIGHEST = lax.Precision.HIGHEST

def view_starts(view_lengths, first_row, count):
    bounds = jnp.cumsum(view_lengths).astype(jnp.int32)[:-1]
    places = first_row + jnp.arange(count, dtype=jnp.int32)
    return jnp.any(places[:, None] == bounds[None, :], axis=1).astype(jnp.float32)

def decays(step_size, starts, decay_rate, view_keep):
    logs = -decay_rate[:, None] * step_size + starts[None, :] * jnp.log(view_keep)[:, None]
    return jnp.cumsum(logs, axis=1)

def span_gram(out_low, in_low):
    return jnp.dot(out_low, jnp.transpose(in_low), preferred_element_type=jnp.float32)

def gram_back(grad_gram, out_rows, in_rows):
    grad_in = jnp.dot(jnp.transpose(grad_gram), out_rows, precision=HIGHEST)
    grad_out = jnp.dot(grad_gram, in_rows, precision=HIGHEST)
    return (grad_in, grad_out)

def span_output(inputs, gram, state_out, step_size, decay_rate, view_keep, skip_gain, carried, starts):
    length = inputs.shape[0]
    cumulative = decays(step_size, starts, decay_rate, view_keep)
    driven = inputs * jnp.transpose(step_size)[:, :, None]
    gaps = cumulative[:, :, None] - cumulative[:, None, :]
    lower = jnp.tril(jnp.ones((length, length), jnp.float32))
    kernel = jnp.exp(jnp.minimum(gaps, 0.0)) * lower[None] * gram[None]
    within = jnp.einsum('hts,shp->thp', kernel, driven, precision=HIGHEST)
    carried_in = jnp.einsum('tn,hpn->thp', state_out, carried, precision=HIGHEST)
    carried_in = carried_in * jnp.exp(jnp.transpose(cumulative))[:, :, None]
    return within + carried_in + skip_gain[None, :, None] * inputs

def span_state(inputs, state_in, step_size, decay_rate, view_keep, starts):
    cumulative = decays(step_size, starts, decay_rate, view_keep)
    driven = inputs * jnp.transpose(step_size)[:, :, None]
    weights = jnp.exp(cumulative[:, -1:] - cumulative)
    state = jnp.einsum('hs,shp,sn->hpn', weights, driven, state_in, precision=HIGHEST)
    return (state, jnp.exp(cumulative[:, -1]))

def output_back(inputs, gram, state_out, step_size, decay_rate, view_keep, skip_gain, carried, starts, cotangent):
    result, pullback = jax.vjp(partial(span_output, starts=starts), inputs, gram, state_out, step_size, decay_rate, view_keep, skip_gain, carried)
    return pullback(cotangent)

def state_back(inputs, state_in, step_size, decay_rate, view_keep, starts, outgoing, total_grad):
    result, pullback = jax.vjp(partial(span_state, starts=starts), inputs, state_in, step_size, decay_rate, view_keep)
    return pullback((outgoing, total_grad))

def scene_attention(queries, key_vectors, values, grad_out, covisible):
    query_blocks = queries.reshape(NBLK, BLK, HEADS, QK)
    key_blocks = key_vectors.reshape(NBLK, BLK, HEADS, QK)
    value_blocks = values.reshape(NBLK, BLK, HEADS, HEAD)
    grad_blocks = grad_out.reshape(NBLK, BLK, HEADS, HEAD)
    score_scale = QK ** (-0.5)

    def one_block(running, block_id):
        key_acc, value_acc = running
        chosen = covisible[block_id]
        key_sel = key_blocks[chosen].reshape(LISTED * BLK, HEADS, QK).astype(jnp.float32)
        value_sel = value_blocks[chosen].reshape(LISTED * BLK, HEADS, HEAD).astype(jnp.float32)
        query_rows = query_blocks[block_id].astype(jnp.float32)
        grad_rows = grad_blocks[block_id].astype(jnp.float32)
        scores = jnp.einsum('ihe,jhe->hij', query_rows, key_sel) * score_scale
        row_top = lax.optimization_barrier(jnp.max(scores, axis=2))
        log_total = row_top + jnp.log(lax.optimization_barrier(jnp.sum(jnp.exp(scores - row_top[:, :, None]), axis=2)))
        attention = jnp.exp(scores - log_total[:, :, None])
        attention_low = lax.optimization_barrier(attention.astype(jnp.bfloat16)).astype(jnp.float32)
        output = jnp.einsum('hij,jhp->ihp', attention_low, value_sel).astype(jnp.bfloat16)
        grad_weights = jnp.einsum('ihp,jhp->hij', grad_rows, value_sel)
        row_delta = lax.optimization_barrier(jnp.sum(attention * grad_weights, axis=2))
        grad_scores = attention * (grad_weights - row_delta[:, :, None]) * score_scale
        grad_scores = lax.optimization_barrier(grad_scores.astype(jnp.bfloat16)).astype(jnp.float32)
        grad_query = jnp.einsum('hij,jhe->ihe', grad_scores, key_sel).astype(jnp.bfloat16)
        key_part = jnp.einsum('hij,ihe->jhe', grad_scores, query_rows).reshape(LISTED, BLK, HEADS, QK)
        value_part = jnp.einsum('hij,ihp->jhp', attention_low, grad_rows).reshape(LISTED, BLK, HEADS, HEAD)
        updated = (key_acc.at[chosen].add(key_part), value_acc.at[chosen].add(value_part))
        return (updated, (output, grad_query))
    start_acc = (jnp.zeros((NBLK, BLK, HEADS, QK), jnp.float32), jnp.zeros((NBLK, BLK, HEADS, HEAD), jnp.float32))
    sums, per_block = lax.scan(one_block, start_acc, jnp.arange(NBLK, dtype=jnp.int32))
    attended = per_block[0].reshape(TOKENS, HEADS * HEAD)
    grad_queries = per_block[1].reshape(TOKENS, HEADS * QK)
    grad_keys = sums[0].reshape(TOKENS, HEADS * QK).astype(jnp.bfloat16)
    grad_values = sums[1].reshape(TOKENS, HEADS, HEAD)
    return (attended, grad_queries, grad_keys, grad_values)

def reference(ssm_input, state_in, state_out, step_size, decay_rate, view_keep, skip_gain, view_lengths, queries, key_vectors, covisible, grad_out):

    def one_scene(scene):
        scene_input, scene_in, scene_out, scene_step, scene_lengths, scene_query, scene_key, scene_lists, scene_grad = scene
        inputs = scene_input.astype(jnp.float32).reshape(N_SEQ, TOK_DEV, HEADS, HEAD)
        in_low = scene_in.reshape(N_SEQ, TOK_DEV, STATE)
        out_low = scene_out.reshape(N_SEQ, TOK_DEV, STATE)
        in_rows = in_low.astype(jnp.float32)
        out_rows = out_low.astype(jnp.float32)
        grams = jax.vmap(span_gram)(out_low, in_low)
        step_rows = jnp.transpose(scene_step.reshape(HEADS, N_SEQ, TOK_DEV), (1, 0, 2))
        firsts = jnp.arange(N_SEQ, dtype=jnp.int32) * TOK_DEV
        starts = jax.vmap(lambda first_row: view_starts(scene_lengths, first_row, TOK_DEV))(firsts)
        states, totals = jax.vmap(span_state, in_axes=(0, 0, 0, None, None, 0))(inputs, in_rows, step_rows, decay_rate, view_keep, starts)
        zero_state = jnp.zeros((HEADS, HEAD, STATE), jnp.float32)

        def link(running, item):
            return (item[0][:, None, None] * running + item[1], running)
        last_state, carried = lax.scan(link, zero_state, (totals, states))
        mixed = jax.vmap(span_output, in_axes=(0, 0, 0, 0, None, None, None, 0, 0))(inputs, grams, out_rows, step_rows, decay_rate, view_keep, skip_gain, carried, starts)
        values = mixed.reshape(TOKENS, HEADS * HEAD).astype(jnp.bfloat16)
        attended, grad_queries, grad_keys, grad_values = scene_attention(scene_query, scene_key, values, scene_grad, scene_lists)
        grad_mixed = grad_values.reshape(N_SEQ, TOK_DEV, HEADS, HEAD)
        out_grads = jax.vmap(output_back, in_axes=(0, 0, 0, 0, None, None, None, 0, 0, 0))(inputs, grams, out_rows, step_rows, decay_rate, view_keep, skip_gain, carried, starts, grad_mixed)
        gram_in, gram_out = jax.vmap(gram_back)(out_grads[1], out_rows, in_rows)
        last_grad, outgoing = lax.scan(link, zero_state, (totals, out_grads[7]), reverse=True)
        total_grads = lax.optimization_barrier(jnp.sum(outgoing * carried, axis=(2, 3)))
        state_grads = jax.vmap(state_back, in_axes=(0, 0, 0, None, None, 0, 0, 0))(inputs, in_rows, step_rows, decay_rate, view_keep, starts, outgoing, total_grads)
        grad_input = (out_grads[0] + state_grads[0]).reshape(TOKENS, HEADS * HEAD).astype(jnp.bfloat16)
        grad_in_rows = (gram_in + state_grads[1]).reshape(TOKENS, STATE).astype(jnp.bfloat16)
        grad_out_rows = (out_grads[2] + gram_out).reshape(TOKENS, STATE).astype(jnp.bfloat16)
        grad_step = jnp.transpose(out_grads[3] + state_grads[2], (1, 0, 2)).reshape(HEADS, TOKENS)
        grad_rate = lax.optimization_barrier(jnp.sum(out_grads[4] + state_grads[3], axis=0))
        grad_keep = lax.optimization_barrier(jnp.sum(out_grads[5] + state_grads[4], axis=0))
        grad_skip = lax.optimization_barrier(jnp.sum(out_grads[6], axis=0))
        return (attended, grad_queries, grad_keys, grad_input, grad_in_rows, grad_out_rows, grad_step, grad_rate, grad_keep, grad_skip)
    results = lax.map(one_scene, (ssm_input, state_in, state_out, step_size, view_lengths, queries, key_vectors, covisible, grad_out))
    return (results[0], results[1], results[2], results[3], results[4], results[5], results[6], lax.optimization_barrier(jnp.sum(results[7], axis=0)), lax.optimization_barrier(jnp.sum(results[8], axis=0)), lax.optimization_barrier(jnp.sum(results[9], axis=0)))
```

```python
from functools import partial

import jax
import jax.numpy as jnp
from jax import lax
from jax.experimental import pallas as pl
from jax.experimental.pallas import tpu as pltpu
from jax.sharding import PartitionSpec as P


BLK = 128
NH = 8
F32 = jnp.float32
BF16 = jnp.bfloat16
MESH = pl.DeviceIdType.MESH
HIGHEST = lax.Precision.HIGHEST

NN = (((1,), (0,)), ((), ()))
NT = (((1,), (1,)), ((), ()))
TN = (((0,), (0,)), ((), ()))


def dot(a, b, dims=NN, precision=None):
    return lax.dot_general(a, b, dims, precision=precision, preferred_element_type=F32)


def halves(a, axis):
    high = a.astype(BF16)
    return jnp.concatenate([high, (a - high.astype(F32)).astype(BF16)], axis=axis)


def twice(a, axis):
    return jnp.concatenate([a, a], axis=axis)


def thirds(a, b, axis):
    a_high, b_high = a.astype(BF16), b.astype(BF16)
    a_rest = (a - a_high.astype(F32)).astype(BF16)
    b_rest = (b - b_high.astype(F32)).astype(BF16)
    return (
        jnp.concatenate([a_high, a_rest, a_high], axis=axis),
        jnp.concatenate([b_high, b_high, b_rest], axis=axis),
    )


def places():
    me = lax.axis_index("seq")
    z = me // 2
    core = lax.rem(me, 2)
    return me, z, core, me // NH, lax.rem(me, NH), me + 1 - 2 * core


def tri(kind):
    row = lax.broadcasted_iota(jnp.int32, (BLK, BLK), 0)
    col = lax.broadcasted_iota(jnp.int32, (BLK, BLK), 1)
    return kind(row, col)


def swap_halves(tile):
    return pltpu.roll(tile.astype(F32), 64, 1).astype(tile.dtype)


def decay_parts(step_tiles, z, core, rate, keep, lengths_ref):
    head = lax.broadcasted_iota(jnp.int32, (NH, NH, BLK), 1)
    step = jnp.sum(jnp.where(head == z, step_tiles, 0.0), axis=1)
    chunk = lax.broadcasted_iota(jnp.int32, (NH, BLK), 0)
    lane = lax.broadcasted_iota(jnp.int32, (NH, BLK), 1)
    place = core * (NH * BLK) + chunk * BLK + lane
    starts = jnp.zeros((NH, BLK), F32)
    bound = jnp.int32(0)
    for v in range(lengths_ref.shape[1] - 1):
        bound = bound + lengths_ref[0, v]
        starts = starts + jnp.where(place == bound, 1.0, 0.0)
    log_keep = jnp.log(jnp.full((NH, BLK), keep, F32))
    logs = starts * log_keep - rate * step
    upper = tri(lambda r, c: jnp.where(r <= c, 1.0, 0.0))
    lower = tri(lambda r, c: jnp.where(r >= c, 1.0, 0.0))
    eye = tri(lambda r, c: jnp.where(r == c, 1.0, 0.0))
    cum_row = dot(logs, upper, NN, HIGHEST)
    cum_col = dot(lower, logs, NT, HIGHEST)
    step_col = dot(eye, step, NT, HIGHEST)
    return step, starts, step_col, cum_row, cum_col


def greet(targets):
    barrier = pltpu.get_barrier_semaphore()
    for target in targets:
        pl.semaphore_signal(barrier, inc=1, device_id=target, device_id_type=MESH)
    pl.semaphore_wait(barrier, len(targets))


def forward_kernel(
    rate_ref, keep_ref, skip_ref, lengths_ref,
    x_ref, b_ref, c_ref, step_ref, q_ref, k_ref, go_ref,
    x_out, b_out, c_out, step_out, qk_out, go_out, v_out, s_out,
    pack, part, sent, got, send_sem, recv_sem, pair_send, pair_recv,
):
    me, z, core, hold_half, hold_slot, partner = places()
    lane = lax.broadcasted_iota(jnp.int32, (BLK, BLK), 1)
    for m in range(NH // 2):
        cols = pl.ds(m * BLK, BLK)
        q_tile, k_tile = q_ref[0, :, cols], k_ref[0, :, cols]
        pack[2 * m] = jnp.where(lane < 64, q_tile, swap_halves(k_tile))
        pack[2 * m + 1] = jnp.where(lane < 64, swap_halves(q_tile), k_tile)

    greet([{"seq": lax.rem(me + o, 2 * NH)} for o in range(1, 2 * NH)])

    def pieces(c):
        cols = pl.ds(pl.multiple_of(c * BLK, BLK), BLK)
        return (
            (x_ref.at[0, :, cols], x_out.at[hold_slot]),
            (b_ref.at[0], b_out.at[hold_slot]),
            (c_ref.at[0], c_out.at[hold_slot]),
            (step_ref.at[0], step_out.at[hold_slot]),
            (pack.at[c], qk_out.at[me]),
            (go_ref.at[0, :, cols], go_out.at[hold_slot]),
        )

    def remote(kind, off):
        c = lax.rem(z + off, NH)
        src, dst = pieces(c)[kind]
        return pltpu.make_async_remote_copy(
            src_ref=src, dst_ref=dst,
            send_sem=send_sem.at[kind, off], recv_sem=recv_sem.at[kind, hold_slot],
            device_id={"seq": 2 * c + hold_half}, device_id_type=MESH,
        )

    def local(kind):
        src, dst = pieces(z)[kind]
        return pltpu.make_async_copy(src, dst, recv_sem.at[kind, hold_slot])

    stay = hold_half == core
    order = (4, 3, 5, 2, 6, 1, 7)
    for kinds in ((0, 1, 2, 3), (4,), (5,)):
        for off in order:
            for kind in kinds:
                remote(kind, off).start()

        @pl.when(stay)
        def _():
            for kind in kinds:
                local(kind).start()

        @pl.when(jnp.logical_not(stay))
        def _():
            for kind in kinds:
                remote(kind, 0).start()

    outs = (x_out, b_out, c_out, step_out, qk_out, go_out)

    def arrived(kind, slot):
        ref = outs[kind].at[core * NH + slot] if kind == 4 else outs[kind].at[slot]
        pltpu.make_async_copy(ref, ref, recv_sem.at[kind, slot]).wait()

    for slot in range(NH):
        for kind in range(4):
            arrived(kind, slot)

    rate, keep, skip = rate_ref[z], keep_ref[z], skip_ref[z]
    step, _, step_col, cum_row, cum_col = decay_parts(
        step_out[...], z, core, rate, keep, lengths_ref
    )
    causal = tri(lambda r, c: r >= c)
    state = jnp.zeros((BLK, BLK), F32)
    for b in range(NH):
        xb, bb, cb = x_out[b], b_out[b], c_out[b]
        a_col, a_row = cum_col[:, b : b + 1], cum_row[b : b + 1, :]
        a_end = cum_row[b : b + 1, BLK - 1 : BLK]
        fade = jnp.where(causal, jnp.exp(jnp.minimum(a_col - a_row, 0.0)), 0.0)
        mix = (fade * dot(cb, bb, NT) * step[b : b + 1, :]).astype(BF16)
        xf = xb.astype(F32)
        part[b] = dot(mix, xb) + skip * xf
        weight = jnp.exp(jnp.minimum(a_end - a_col, 0.0)) * step_col[:, b : b + 1]
        s_out[b] = state
        state = jnp.exp(a_end) * state + dot(twice(bb, 0), halves(xf * weight, 0), TN)
    sent[...] = state

    def pair(src, dst, i):
        return pltpu.make_async_remote_copy(
            src_ref=src, dst_ref=dst, send_sem=pair_send.at[i], recv_sem=pair_recv.at[i],
            device_id={"seq": partner}, device_id_type=MESH,
        )

    state_copy = pair(sent, got, 0)
    state_copy.start()
    state_copy.wait()
    entering = got[...] * jnp.where(core == 1, 1.0, 0.0)
    before = jnp.zeros((1, 1), F32)
    for b in range(NH):
        carried = s_out[b] + jnp.exp(before) * entering
        s_out[b] = carried
        moved = dot(c_out[b], carried.astype(BF16))
        value = part[b] + jnp.exp(cum_col[:, b : b + 1]) * moved
        v_out[core * NH + b] = value.astype(BF16)
        before = before + cum_row[b : b + 1, BLK - 1 : BLK]

    mine = pl.ds(pl.multiple_of(core * NH, NH), NH)
    value_copy = pair(v_out.at[mine], v_out.at[mine], 1)
    value_copy.start()
    for slot in range(NH):
        arrived(4, slot)
    key_copy = pair(qk_out.at[mine], qk_out.at[mine], 2)
    key_copy.start()
    for slot in range(NH):
        arrived(5, slot)
    value_copy.wait()
    key_copy.wait()
    for kind in range(6):
        for off in order:
            remote(kind, off).wait_send()

    @pl.when(jnp.logical_not(stay))
    def _():
        for kind in range(6):
            remote(kind, 0).wait_send()


def attention_kernel(
    lists_ref, qk_ref, go_ref, v_ref,
    att_out, dq_out, dv_own, dv_other, dk_own, dk_other,
    dv_acc, dk_acc,
):
    core = lax.rem(lax.axis_index("seq"), 2)
    lane = lax.broadcasted_iota(jnp.int32, (BLK, BLK), 1)
    low = lane < 64
    dv_acc[...] = jnp.zeros_like(dv_acc)
    dk_acc[...] = jnp.zeros_like(dk_acc)

    def one(b, carry):
        block = core * NH + b
        listed = [lists_ref[0, block, i] for i in range(4)]
        qk = qk_ref[block]
        zero = jnp.zeros_like(qk)
        q_high = (pltpu.roll(qk.astype(F32), 64, 1) * 0.125).astype(BF16)
        q_low = jnp.where(low, qk, zero)
        keys = jnp.concatenate([jnp.where(low, zero, qk_ref[j]) for j in listed], axis=0)
        values = jnp.concatenate([v_ref[j] for j in listed], axis=0)
        grad = go_ref[b]
        scores = dot(keys, q_high, NT)
        top = jnp.max(scores, axis=0, keepdims=True)
        weights = jnp.exp(scores - top)
        weights = weights * (1.0 / jnp.sum(weights, axis=0, keepdims=True))
        weights_low = weights.astype(BF16)
        att_out[b] = dot(weights_low, values, TN).astype(BF16)
        dweights = dot(values, grad, NT)
        delta = jnp.sum(weights * dweights, axis=0, keepdims=True)
        dscores = (weights * (dweights - delta) * 0.125).astype(BF16)
        dq_out[b] = dot(dscores, keys, TN).astype(BF16)
        dvalues = dot(weights_low, grad)
        dkeys = dot(dscores, q_low)
        for i, j in enumerate(listed):
            rows = slice(i * BLK, (i + 1) * BLK)
            dv_acc[j] += dvalues[rows]
            dk_acc[j] += dkeys[rows]
        return carry

    lax.fori_loop(0, NH, one, 0)
    mine = pl.ds(core * NH, NH)
    other = pl.ds((1 - core) * NH, NH)
    dv_own[...] = dv_acc[mine]
    dk_own[...] = dk_acc[mine]
    dv_other[...] = dv_acc[other]
    dk_other[...] = dk_acc[other].astype(BF16)


def backward_kernel(
    nx, ny,
    rate_ref, keep_ref, skip_ref, lengths_ref,
    x_ref, b_ref, c_ref, step_ref, s_ref,
    att_ref, dq_ref, dv_own, dv_other, dk_own, dk_other,
    att_out, dx_out, dq_out, dk_out, db_out, dc_out, dstep_out, par_out,
    dv_got, dk_got, dqk, dqk_got, dx, dbc, dbc_got, dst, dst_got,
    chain, sent, got, par_x, par_y, par_z,
    send_sem, recv_sem, pair_send, pair_recv, x_send, x_recv, y_send, y_recv, z_send, z_recv,
):
    me, z, core, hold_half, hold_slot, partner = places()
    dp = lax.axis_index("dp")
    at_x, at_y = lax.rem(dp, nx), dp // nx
    x_peers = [at_y * nx + lax.rem(at_x + o, nx) for o in range(1, nx)]
    y_peers = [lax.rem(at_y + o, ny) * nx + at_x for o in range(1, ny)]
    z_peers = [lax.rem(me + o, 2 * NH) for o in range(1, 2 * NH)]
    greet(
        [{"seq": peer} for peer in z_peers] + [{"dp": peer} for peer in x_peers + y_peers]
    )

    head_cols = pl.ds(pl.multiple_of(z * BLK, BLK), BLK)

    def piece(kind, b):
        return (
            (att_ref.at[b], att_out.at[0, :, head_cols]),
            (dqk.at[b], dqk_got.at[z]),
            (dx.at[b], dx_out.at[0, :, head_cols]),
            (dbc.at[b], dbc_got.at[z]),
            (dst.at[b], dst_got.at[z]),
        )[kind]

    def remote(kind, b):
        src, dst_ref = piece(kind, b)
        return pltpu.make_async_remote_copy(
            src_ref=src, dst_ref=dst_ref,
            send_sem=send_sem.at[kind, b], recv_sem=recv_sem.at[kind, z],
            device_id={"seq": core * NH + b}, device_id_type=MESH,
        )

    def start(kind, b):
        stay = core * NH + b == me

        @pl.when(stay)
        def _():
            src, dst_ref = piece(kind, b)
            pltpu.make_async_copy(src, dst_ref, recv_sem.at[kind, z]).start()

        @pl.when(jnp.logical_not(stay))
        def _():
            remote(kind, b).start()

    def pair(src, dst_ref, i):
        return pltpu.make_async_remote_copy(
            src_ref=src, dst_ref=dst_ref, send_sem=pair_send.at[i], recv_sem=pair_recv.at[i],
            device_id={"seq": partner}, device_id_type=MESH,
        )

    dv_copy = pair(dv_other, dv_got, 0)
    dv_copy.start()
    dk_copy = pair(dk_other, dk_got, 1)
    dk_copy.start()
    for off in range(NH):
        start(0, lax.rem(hold_slot + off, NH))

    rate, keep, skip = rate_ref[z], keep_ref[z], skip_ref[z]
    step, starts, step_col, cum_row, cum_col = decay_parts(
        step_ref[...], z, core, rate, keep, lengths_ref
    )
    dv_copy.wait()
    tail = jnp.zeros((BLK, BLK), F32)
    for b in reversed(range(NH)):
        dy = dv_own[b] + dv_got[b]
        chain[b] = tail
        a_end = cum_row[b : b + 1, BLK - 1 : BLK]
        scaled = halves(dy * jnp.exp(cum_col[:, b : b + 1]), 0)
        tail = jnp.exp(a_end) * tail + dot(twice(c_ref[b], 0), scaled, TN)
    sent[...] = tail
    state_copy = pair(sent, got, 2)
    state_copy.start()
    dk_copy.wait()
    for b in range(NH):
        both = dk_own[b] + dk_got[b].astype(F32) + dq_ref[b].astype(F32)
        dqk[b] = both.astype(BF16)
    for off in range(NH):
        start(1, lax.rem(hold_slot + off, NH))
    state_copy.wait()
    leaving = got[...] * jnp.where(core == 0, 1.0, 0.0)

    causal = tri(lambda r, c: r >= c)
    same = tri(lambda r, c: r == c)
    strict = twice(tri(lambda r, c: jnp.where(r < c, 1.0, 0.0)).astype(BF16), 0)
    after = jnp.zeros((1, 1), F32)
    drate = jnp.zeros((1, BLK), F32)
    dkeep = jnp.zeros((1, BLK), F32)
    dskip = jnp.zeros((1, BLK), F32)
    for b in reversed(range(NH)):
        xb, bb, cb = x_ref[b], b_ref[b], c_ref[b]
        xf, bf, cf = xb.astype(F32), bb.astype(F32), cb.astype(F32)
        dy = dv_own[b] + dv_got[b]
        dy_low = dy.astype(BF16)
        a_col, a_row = cum_col[:, b : b + 1], cum_row[b : b + 1, :]
        a_end = cum_row[b : b + 1, BLK - 1 : BLK]
        s_col, s_row = step_col[:, b : b + 1], step[b : b + 1, :]
        later = chain[b] + jnp.exp(after) * leaving
        later_low = later.astype(BF16)
        carried = s_ref[b]
        after = after + a_end
        fade = jnp.where(causal, jnp.exp(jnp.minimum(a_col - a_row, 0.0)), 0.0)
        gram = dot(cb, bb, NT)
        dgram = fade * s_row * dot(halves(dy, 1), twice(xb, 1), NT)
        dgram_low = dgram.astype(BF16)
        to_end = jnp.exp(jnp.minimum(a_end - a_col, 0.0))
        du = dot((fade * gram).astype(BF16), dy_low, TN) + to_end * dot(bb, later_low)
        dx[b] = (s_col * du + skip * dy).astype(BF16)
        dc_far = jnp.exp(a_col) * dot(*thirds(dy, carried, 1), NT)
        db_far = to_end * s_col * dot(twice(xb, 1), halves(later, 1), NT)
        dbc[b, :, 0:BLK] = (dot(dgram_low, cb, TN) + db_far).astype(BF16)
        dbc[b, :, BLK : 2 * BLK] = (dot(dgram_low, bb) + dc_far).astype(BF16)
        crossing = dot(halves(gram * dgram, 1), strict)
        far_out = jnp.sum(cf * dc_far, axis=1, keepdims=True)
        far_in = jnp.sum(bf * db_far, axis=1, keepdims=True)
        dlog = jnp.sum(jnp.where(causal, crossing + far_out, far_in), axis=0, keepdims=True)
        dlog = dlog + jnp.exp(a_end) * jnp.sum(later * carried)
        direct = jnp.sum(xf * du, axis=1, keepdims=True)
        direct = jnp.sum(jnp.where(same, direct, 0.0), axis=0, keepdims=True)
        dst[b] = jnp.broadcast_to(direct - rate * dlog, (NH, BLK))
        drate = drate - s_row * dlog
        dkeep = dkeep + starts[b : b + 1, :] * dlog
        dskip = dskip + jnp.sum(dy * xf, axis=0, keepdims=True)
        for kind in (2, 3, 4):
            start(kind, b)

    lane = lax.broadcasted_iota(jnp.int32, (NH, BLK), 1)
    dkeep = jnp.sum(dkeep, axis=1, keepdims=True) / jnp.full((1, 1), keep, F32)
    drate = jnp.sum(drate, axis=1, keepdims=True)
    dskip = jnp.sum(dskip, axis=1, keepdims=True)
    tile = jnp.where(lane == 0, drate, jnp.where(lane == 1, dkeep, jnp.where(lane == 2, dskip, 0.0)))

    def spread(tile, buf, place, axis, peers, sems, rsems):
        buf[place] = tile
        copies = []
        for i, peer in enumerate(peers):
            copy = pltpu.make_async_remote_copy(
                src_ref=buf.at[place], dst_ref=buf.at[place],
                send_sem=sems.at[i], recv_sem=rsems.at[place],
                device_id={axis: peer}, device_id_type=MESH,
            )
            copy.start()
            copies.append(copy)
        return copies

    def gathered(buf, place, count, copies, rsems):
        for o in range(1, count):
            source = lax.rem(place + o, count)
            ref = buf.at[source]
            pltpu.make_async_copy(ref, ref, rsems.at[source]).wait()
        for copy in copies:
            copy.wait_send()

    copies = spread(tile, par_x, at_x, "dp", x_peers, x_send, x_recv)
    gathered(par_x, at_x, nx, copies, x_recv)
    copies = spread(jnp.sum(par_x[...], axis=0), par_y, at_y, "dp", y_peers, y_send, y_recv)
    gathered(par_y, at_y, ny, copies, y_recv)
    z_copies = spread(jnp.sum(par_y[...], axis=0), par_z, me, "seq", z_peers, z_send, z_recv)

    def arrived(kind, c):
        cols = pl.ds(c * BLK, BLK)
        ref = (
            att_out.at[0, :, cols], dqk_got.at[c], dx_out.at[0, :, cols], dbc_got.at[c],
            dst_got.at[c],
        )[kind]
        pltpu.make_async_copy(ref, ref, recv_sem.at[kind, c]).wait()

    for c in range(NH):
        arrived(1, c)
    low = lax.broadcasted_iota(jnp.int32, (BLK, BLK), 1) < 64
    for m in range(NH // 2):
        even, odd = dqk_got[2 * m], dqk_got[2 * m + 1]
        cols = pl.ds(m * BLK, BLK)
        dq_out[0, :, cols] = jnp.where(low, swap_halves(even), odd)
        dk_out[0, :, cols] = jnp.where(low, even, swap_halves(odd))
    for c in range(NH):
        for kind in (0, 2, 3, 4):
            arrived(kind, c)
    total = jnp.zeros((BLK, 2 * BLK), F32)
    for c in range(NH):
        total = total + dbc_got[c].astype(F32)
        dstep_out[0, c : c + 1, :] = dst_got[c, 0:1, :]
    db_out[0] = total[:, 0:BLK].astype(BF16)
    dc_out[0] = total[:, BLK : 2 * BLK].astype(BF16)
    gathered(par_z, me, 2 * NH, z_copies, z_recv)
    for c in range(NH):
        par_out[c : c + 1, :] = par_z[2 * c, 0:1, :] + par_z[2 * c + 1, 0:1, :]
    for kind in range(5):
        for b in range(NH):

            @pl.when(core * NH + b != me)
            def _():
                remote(kind, b).wait_send()


VM = pl.BlockSpec(memory_space=pltpu.VMEM)
SM = pl.BlockSpec(memory_space=pltpu.SMEM)


def per_device(
    nx, ny, x, b_in, c_out, step, rate, keep, skip, lengths, q, k, lists, go
):
    def arr(*shape, dtype=BF16):
        return jax.ShapeDtypeStruct(shape, dtype)

    sq = (BLK, BLK)
    dma = pltpu.SemaphoreType.DMA
    xs, bs, cs, steps, qks, gos, vs, states = pl.pallas_call(
        forward_kernel,
        out_shape=(
            arr(NH, *sq), arr(NH, *sq), arr(NH, *sq), arr(NH, NH, BLK, dtype=F32),
            arr(2 * NH, *sq), arr(NH, *sq), arr(2 * NH, *sq), arr(NH, *sq, dtype=F32),
        ),
        in_specs=[SM] * 4 + [VM] * 7,
        out_specs=(VM,) * 8,
        scratch_shapes=[
            pltpu.VMEM((NH, *sq), BF16), pltpu.VMEM((NH, *sq), F32),
            pltpu.VMEM(sq, F32), pltpu.VMEM(sq, F32),
            dma((6, NH)), dma((6, NH)), dma((3,)), dma((3,)),
        ],
        compiler_params=pltpu.CompilerParams(collective_id=0, has_side_effects=True),
        name="exchange_forward",
    )(rate, keep, skip, lengths, x, b_in, c_out, step, q, k, go)
    att, dq, dv_own, dv_other, dk_own, dk_other = pl.pallas_call(
        attention_kernel,
        out_shape=(
            arr(NH, *sq), arr(NH, *sq), arr(NH, *sq, dtype=F32), arr(NH, *sq, dtype=F32),
            arr(NH, *sq, dtype=F32), arr(NH, *sq),
        ),
        in_specs=[SM] + [VM] * 3,
        out_specs=(VM,) * 6,
        scratch_shapes=[pltpu.VMEM((2 * NH, *sq), F32), pltpu.VMEM((2 * NH, *sq), F32)],
        name="attention",
    )(lists, qks, gos, vs)
    outs = pl.pallas_call(
        partial(backward_kernel, nx, ny),
        out_shape=(
            arr(1, BLK, NH * BLK), arr(1, BLK, NH * BLK), arr(1, BLK, NH * 64),
            arr(1, BLK, NH * 64), arr(1, *sq), arr(1, *sq), arr(1, NH, BLK, dtype=F32),
            arr(NH, BLK, dtype=F32),
        ),
        in_specs=[SM] * 4 + [VM] * 11,
        out_specs=(VM,) * 8,
        scratch_shapes=[
            pltpu.VMEM((NH, *sq), F32), pltpu.VMEM((NH, *sq), BF16),
            pltpu.VMEM((NH, *sq), BF16), pltpu.VMEM((NH, *sq), BF16),
            pltpu.VMEM((NH, *sq), BF16),
            pltpu.VMEM((NH, BLK, 2 * BLK), BF16), pltpu.VMEM((NH, BLK, 2 * BLK), BF16),
            pltpu.VMEM((NH, NH, BLK), F32), pltpu.VMEM((NH, NH, BLK), F32),
            pltpu.VMEM((NH, *sq), F32), pltpu.VMEM(sq, F32), pltpu.VMEM(sq, F32),
            pltpu.VMEM((nx, NH, BLK), F32), pltpu.VMEM((ny, NH, BLK), F32),
            pltpu.VMEM((2 * NH, NH, BLK), F32),
            dma((5, NH)), dma((5, NH)), dma((3,)), dma((3,)),
            dma((nx,)), dma((nx,)), dma((ny,)), dma((ny,)), dma((2 * NH,)), dma((2 * NH,)),
        ],
        compiler_params=pltpu.CompilerParams(collective_id=1, has_side_effects=True),
        name="backward_exchange",
    )(rate, keep, skip, lengths, xs, bs, cs, steps, states,
      att, dq, dv_own, dv_other, dk_own, dk_other)
    att, dx, dq, dk, db, dc, dstep, par = outs
    return att, dq, dk, dx, db, dc, dstep, par[:, 0], par[:, 1], par[:, 2]


def solution(mesh):
    rows = P("dp", "seq", None)
    heads = P("dp", None, "seq")
    scene = P("dp", None)
    in_specs = (
        rows, rows, rows, heads, P(), P(), P(), scene, rows, rows, P("dp", None, None), rows,
    )
    out_specs = (rows,) * 6 + (heads, P(), P(), P())
    nx = 4 if mesh.shape["dp"] % 4 == 0 else 1
    ny = mesh.shape["dp"] // nx
    return jax.shard_map(
        partial(per_device, nx, ny), mesh=mesh, in_specs=in_specs, out_specs=out_specs,
        check_vma=False,
    )
```

```python
from functools import partial

import jax
import jax.numpy as jnp
from jax import lax
from jax.experimental import pallas as pl
from jax.experimental.pallas import tpu as pltpu
from jax.sharding import PartitionSpec as P


BLK = 128
NH = 8
LISTED = 4
F32 = jnp.float32
BF16 = jnp.bfloat16
MESH = pl.DeviceIdType.MESH
HIGHEST = lax.Precision.HIGHEST

NN = (((1,), (0,)), ((), ()))
NT = (((1,), (1,)), ((), ()))
TN = (((0,), (0,)), ((), ()))

X, B, C, STEP, QK, GO = range(6)
ATT, DQK, DX, DBC, DST = range(5)


def dot(a, b, dims=NN, precision=None):
    return lax.dot_general(a, b, dims, precision=precision, preferred_element_type=F32)


def halves(a, axis):
    high = a.astype(BF16)
    return jnp.concatenate([high, (a - high.astype(F32)).astype(BF16)], axis=axis)


def twice(a, axis):
    return jnp.concatenate([a, a], axis=axis)


def thirds(a, b, axis):
    a_high, b_high = a.astype(BF16), b.astype(BF16)
    a_rest = (a - a_high.astype(F32)).astype(BF16)
    b_rest = (b - b_high.astype(F32)).astype(BF16)
    return (
        jnp.concatenate([a_high, a_rest, a_high], axis=axis),
        jnp.concatenate([b_high, b_high, b_rest], axis=axis),
    )


def tri(kind):
    row = lax.broadcasted_iota(jnp.int32, (BLK, BLK), 0)
    col = lax.broadcasted_iota(jnp.int32, (BLK, BLK), 1)
    return kind(row, col)


def swap_halves(tile):
    return pltpu.roll(tile.astype(F32), 64, 1).astype(tile.dtype)


def decay_parts(step_tiles, z, core, rate, keep, lengths_ref):
    head = lax.broadcasted_iota(jnp.int32, (NH, NH, BLK), 1)
    step = jnp.sum(jnp.where(head == z, step_tiles, 0.0), axis=1)
    chunk = lax.broadcasted_iota(jnp.int32, (NH, BLK), 0)
    lane = lax.broadcasted_iota(jnp.int32, (NH, BLK), 1)
    place = core * (NH * BLK) + chunk * BLK + lane
    starts = jnp.zeros((NH, BLK), F32)
    bound = jnp.int32(0)
    for v in range(lengths_ref.shape[1] - 1):
        bound = bound + lengths_ref[0, v]
        starts = starts + jnp.where(place == bound, 1.0, 0.0)
    log_keep = jnp.log(jnp.full((NH, BLK), keep, F32))
    logs = starts * log_keep - rate * step
    upper = tri(lambda r, c: jnp.where(r <= c, 1.0, 0.0))
    lower = tri(lambda r, c: jnp.where(r >= c, 1.0, 0.0))
    eye = tri(lambda r, c: jnp.where(r == c, 1.0, 0.0))
    cum_row = dot(logs, upper, NN, HIGHEST)
    cum_col = dot(lower, logs, NT, HIGHEST)
    step_col = dot(eye, step, NT, HIGHEST)
    return step, starts, step_col, cum_row, cum_col


def greet(targets):
    barrier = pltpu.get_barrier_semaphore()
    for target in targets:
        pl.semaphore_signal(barrier, inc=1, device_id=target, device_id_type=MESH)
    pl.semaphore_wait(barrier, len(targets))


def main_kernel(
    nx, ny,
    rate_ref, keep_ref, skip_ref, lengths_ref, lists_ref,
    x_ref, b_ref, c_ref, step_ref, q_ref, k_ref, go_ref,
    att_got, dx_got, dqk_got, dbc_got, dst_got, par_z,
    pack, xs, bs, cs, steps, qks, gos, vs, states, fades, mixes, part,
    sent, got, att, dqs, dv_parts, dk_parts, dv, dv_out, dv_in, dk, dk_out, dk_in,
    chain, dqk, dx, dbc, dst, par_x, par_y, par_mine,
    in_send, in_recv, hop_send, pair_send, pair_recv, out_send, out_recv,
    x_send, x_recv, y_send, y_recv, z_send, z_recv,
):
    me = lax.axis_index("seq")
    z, core = me // 2, lax.rem(me, 2)
    hold_half, hold_slot = me // NH, lax.rem(me, NH)
    partner = me + 1 - 2 * core
    dp = lax.axis_index("dp")
    at_x, at_y = lax.rem(dp, nx), dp // nx
    x_peers = [at_y * nx + lax.rem(at_x + o, nx) for o in range(1, nx)]
    y_peers = [lax.rem(at_y + o, ny) * nx + at_x for o in range(1, ny)]
    z_peers = [lax.rem(me + o, 2 * NH) for o in range(1, 2 * NH)]

    tile_lane = lax.broadcasted_iota(jnp.int32, (BLK, BLK), 1)
    low = tile_lane < 64
    for m in range(NH // 2):
        cols = pl.ds(m * BLK, BLK)
        q_tile, k_tile = q_ref[0, :, cols], k_ref[0, :, cols]
        pack[2 * m] = jnp.where(low, q_tile, swap_halves(k_tile))
        pack[2 * m + 1] = jnp.where(low, swap_halves(q_tile), k_tile)

    greet(
        [{"seq": peer} for peer in z_peers] + [{"dp": peer} for peer in x_peers + y_peers]
    )

    ins = (xs, bs, cs, steps, qks, gos)

    def in_piece(kind, c):
        cols = pl.ds(pl.multiple_of(c * BLK, BLK), BLK)
        return (
            (x_ref.at[0, :, cols], xs.at[hold_slot]),
            (b_ref.at[0], bs.at[hold_slot]),
            (c_ref.at[0], cs.at[hold_slot]),
            (step_ref.at[0], steps.at[hold_slot]),
            (pack.at[c], qks.at[me]),
            (go_ref.at[0, :, cols], gos.at[hold_slot]),
        )[kind]

    def in_remote(kind, off):
        c = lax.rem(z + off, NH)
        src, dst_ref = in_piece(kind, c)
        return pltpu.make_async_remote_copy(
            src_ref=src, dst_ref=dst_ref,
            send_sem=in_send.at[kind, off], recv_sem=in_recv.at[kind, hold_slot],
            device_id={"seq": 2 * c + hold_half}, device_id_type=MESH,
        )

    stay = hold_half == core
    offsets = {kind: (4, 3, 5, 2, 6, 1, 7) for kind in range(6)}
    offsets[B] = offsets[C] = (1, 7)

    def send_in(kinds):
        for off in (4, 3, 5, 2, 6, 1, 7):
            for kind in kinds:
                if off in offsets[kind]:
                    in_remote(kind, off).start()

        @pl.when(stay)
        def _():
            for kind in kinds:
                src, dst_ref = in_piece(kind, z)
                pltpu.make_async_copy(src, dst_ref, in_recv.at[kind, hold_slot]).start()

        @pl.when(jnp.logical_not(stay))
        def _():
            for kind in kinds:
                in_remote(kind, 0).start()

    def came(kind, slot):
        ref = ins[kind].at[core * NH + slot] if kind == QK else ins[kind].at[slot]
        pltpu.make_async_copy(ref, ref, in_recv.at[kind, slot]).wait()

    def hop(kind, dist, sign, j):
        source = lax.rem(z - sign * dist + NH, NH)
        slot = 2 * lax.rem(source, NH // 2) + j
        ref = ins[kind].at[slot]
        return pltpu.make_async_remote_copy(
            src_ref=ref, dst_ref=ref,
            send_sem=hop_send.at[kind - B, (dist - 1) * 2 + (1 - sign) // 2, j],
            recv_sem=in_recv.at[kind, slot],
            device_id={"seq": lax.rem(me + 2 * sign + 2 * NH, 2 * NH)}, device_id_type=MESH,
        )

    hops = [
        (dist, sign, [k for k, reach in ((B, 4 if sign > 0 else 3), (C, 3 if sign > 0 else 4))
                      if dist < reach])
        for dist in (1, 2, 3) for sign in (1, -1)
    ]

    def from_half(dist, sign):
        return lax.rem(z - sign * dist + NH, NH) // (NH // 2) == core

    send_in((B, C))
    send_in((X, STEP))
    for dist, sign, onward in hops:

        @pl.when(from_half(dist, sign))
        def _():
            source = lax.rem(z - sign * dist + NH, NH)
            for j in range(2):
                for kind in (B, C):
                    came(kind, 2 * lax.rem(source, NH // 2) + j)
                    if kind in onward:
                        hop(kind, dist, sign, j).start()

    send_in((QK,))
    send_in((GO,))
    for dist in (0, 4):

        @pl.when(from_half(dist, 1))
        def _():
            source = lax.rem(z + dist, NH)
            for j in range(2):
                for kind in (B, C):
                    came(kind, 2 * lax.rem(source, NH // 2) + j)

    for slot in range(NH):
        came(X, slot)
        came(STEP, slot)

    rate, keep, skip = rate_ref[z], keep_ref[z], skip_ref[z]
    step, starts, step_col, cum_row, cum_col = decay_parts(
        steps[...], z, core, rate, keep, lengths_ref
    )
    causal = tri(lambda r, c: r >= c)

    def chunk_decay(b):
        a_col, a_row = cum_col[:, b : b + 1], cum_row[b : b + 1, :]
        return a_col, a_row, cum_row[b : b + 1, BLK - 1 : BLK]

    state = jnp.zeros((BLK, BLK), F32)
    for b in range(NH):
        xb, bb, cb = xs[b], bs[b], cs[b]
        a_col, a_row, a_end = chunk_decay(b)
        xf = xb.astype(F32)
        weight = jnp.exp(jnp.minimum(a_end - a_col, 0.0)) * step_col[:, b : b + 1]
        states[b] = state
        state = jnp.exp(a_end) * state + dot(twice(bb, 0), halves(xf * weight, 0), TN)
    sent[...] = state

    def pair(src, dst_ref, i):
        return pltpu.make_async_remote_copy(
            src_ref=src, dst_ref=dst_ref, send_sem=pair_send.at[i], recv_sem=pair_recv.at[i],
            device_id={"seq": partner}, device_id_type=MESH,
        )

    state_copy = pair(sent, got, 0)
    state_copy.start()
    for b in range(NH):
        xb, bb, cb = xs[b], bs[b], cs[b]
        a_col, a_row, a_end = chunk_decay(b)
        fade = jnp.where(causal, jnp.exp(jnp.minimum(a_col - a_row, 0.0)), 0.0)
        fades[b] = fade
        mix = fade * dot(cb, bb, NT)
        mixes[b] = mix
        part[b] = dot((mix * step[b : b + 1, :]).astype(BF16), xb) + skip * xb.astype(F32)
    state_copy.wait()
    entering = got[...] * jnp.where(core == 1, 1.0, 0.0)
    before = jnp.zeros((1, 1), F32)
    for b in range(NH):
        a_col, a_row, a_end = chunk_decay(b)
        carried = states[b] + jnp.exp(before) * entering
        states[b] = carried
        value = part[b] + jnp.exp(a_col) * dot(cs[b], carried.astype(BF16))
        vs[core * NH + b] = value.astype(BF16)
        before = before + a_end

    mine = pl.ds(pl.multiple_of(core * NH, NH), NH)
    value_copy = pair(vs.at[mine], vs.at[mine], 1)
    value_copy.start()
    for slot in range(NH):
        came(QK, slot)
    key_copy = pair(qks.at[mine], qks.at[mine], 2)
    key_copy.start()
    value_copy.wait()
    key_copy.wait()

    head_cols = pl.ds(pl.multiple_of(z * BLK, BLK), BLK)

    def out_piece(kind, b):
        return (
            (att.at[b], att_got.at[0, :, head_cols]),
            (dqk.at[b], dqk_got.at[z]),
            (dx.at[b], dx_got.at[0, :, head_cols]),
            (dbc.at[b], dbc_got.at[z]),
            (dst.at[b], dst_got.at[z]),
        )[kind]

    def out_remote(kind, b):
        src, dst_ref = out_piece(kind, b)
        return pltpu.make_async_remote_copy(
            src_ref=src, dst_ref=dst_ref,
            send_sem=out_send.at[kind, b], recv_sem=out_recv.at[kind, z],
            device_id={"seq": core * NH + b}, device_id_type=MESH,
        )

    def send_out(kinds, b):
        here = core * NH + b == me

        @pl.when(here)
        def _():
            for kind in kinds:
                src, dst_ref = out_piece(kind, b)
                pltpu.make_async_copy(src, dst_ref, out_recv.at[kind, z]).start()

        @pl.when(jnp.logical_not(here))
        def _():
            for kind in kinds:
                out_remote(kind, b).start()

    def one(b, carry):
        came(GO, b)
        block = core * NH + b
        listed = [lists_ref[0, block, i] for i in range(LISTED)]
        qk = qks[block]
        zero = jnp.zeros_like(qk)
        q_high = (pltpu.roll(qk.astype(F32), 64, 1) * 0.125).astype(BF16)
        q_low = jnp.where(low, qk, zero)
        keys = jnp.concatenate([jnp.where(low, zero, qks[j]) for j in listed], axis=0)
        values = jnp.concatenate([vs[j] for j in listed], axis=0)
        grad = gos[b]
        scores = dot(keys, q_high, NT)
        top = jnp.max(scores, axis=0, keepdims=True)
        weights = jnp.exp(scores - top)
        weights = weights * (1.0 / jnp.sum(weights, axis=0, keepdims=True))
        weights_low = weights.astype(BF16)
        att[b] = dot(weights_low, values, TN).astype(BF16)
        send_out((ATT,), b)
        dweights = dot(values, grad, NT)
        delta = jnp.sum(weights * dweights, axis=0, keepdims=True)
        dscores = (weights * (dweights - delta) * 0.125).astype(BF16)
        dqs[b] = dot(dscores, keys, TN).astype(BF16)
        dv_parts[pl.ds(b * LISTED, LISTED)] = dot(weights_low, grad).reshape(LISTED, BLK, BLK)
        dk_parts[pl.ds(b * LISTED, LISTED)] = dot(dscores, q_low).reshape(LISTED, BLK, BLK)
        return carry

    lax.fori_loop(0, NH, one, 0)

    def key_sums(j, keep_dv, keep_dk):
        dv_sum = jnp.zeros((BLK, BLK), F32)
        dk_sum = jnp.zeros((BLK, BLK), F32)
        for b in range(NH):
            slot = jnp.int32(0)
            lists = jnp.int32(0)
            for i in range(LISTED):
                hit = (lists_ref[0, core * NH + b, i] == j).astype(jnp.int32)
                slot = slot + i * hit
                lists = lists + hit
            slot = jnp.minimum(slot, LISTED - 1)
            share = lists.astype(F32)
            dv_sum = dv_sum + share * dv_parts[b * LISTED + slot]
            dk_sum = dk_sum + share * dk_parts[b * LISTED + slot]
        keep_dv(dv_sum)
        keep_dk(dk_sum)

    def for_partner(j, carry):
        def keep_dv(a):
            dv_out[j] = a

        def keep_dk(a):
            dk_out[j] = a.astype(BF16)

        key_sums((1 - core) * NH + j, keep_dv, keep_dk)
        return carry

    def for_me(j, carry):
        def keep_dv(a):
            dv[j] = a

        def keep_dk(a):
            dk[j] = a

        key_sums(core * NH + j, keep_dv, keep_dk)
        return carry

    lax.fori_loop(0, NH, for_partner, 0)
    dv_copy = pair(dv_out, dv_in, 3)
    dv_copy.start()
    dk_copy = pair(dk_out, dk_in, 4)
    dk_copy.start()
    lax.fori_loop(0, NH, for_me, 0)
    dv_copy.wait()

    tail = jnp.zeros((BLK, BLK), F32)
    for b in reversed(range(NH)):
        a_col, a_row, a_end = chunk_decay(b)
        dy = dv[b] + dv_in[b]
        dv[b] = dy
        chain[b] = tail
        tail = jnp.exp(a_end) * tail + dot(twice(cs[b], 0), halves(dy * jnp.exp(a_col), 0), TN)
    sent[...] = tail
    tail_copy = pair(sent, got, 5)
    tail_copy.start()
    dk_copy.wait()
    for b in range(NH):
        dqk[b] = (dk[b] + dk_in[b].astype(F32) + dqs[b].astype(F32)).astype(BF16)
    for off in range(NH):
        send_out((DQK,), lax.rem(hold_slot + off, NH))
    tail_copy.wait()
    leaving = got[...] * jnp.where(core == 0, 1.0, 0.0)

    same = tri(lambda r, c: r == c)
    strict = twice(tri(lambda r, c: jnp.where(r < c, 1.0, 0.0)).astype(BF16), 0)
    after = jnp.zeros((1, 1), F32)
    drate = jnp.zeros((1, BLK), F32)
    dkeep = jnp.zeros((1, BLK), F32)
    dskip = jnp.zeros((1, BLK), F32)
    for b in reversed(range(NH)):
        xb, bb, cb = xs[b], bs[b], cs[b]
        xf, bf, cf = xb.astype(F32), bb.astype(F32), cb.astype(F32)
        dy = dv[b]
        a_col, a_row, a_end = chunk_decay(b)
        s_col, s_row = step_col[:, b : b + 1], step[b : b + 1, :]
        later = chain[b] + jnp.exp(after) * leaving
        later_low = later.astype(BF16)
        carried = states[b]
        after = after + a_end
        mix = mixes[b]
        dmix = s_row * dot(halves(dy, 1), twice(xb, 1), NT)
        dgram_low = (fades[b] * dmix).astype(BF16)
        to_end = jnp.exp(jnp.minimum(a_end - a_col, 0.0))
        du = dot(mix.astype(BF16), dy.astype(BF16), TN) + to_end * dot(bb, later_low)
        dx[b] = (s_col * du + skip * dy).astype(BF16)
        dc_far = jnp.exp(a_col) * dot(*thirds(dy, carried, 1), NT)
        db_far = to_end * s_col * dot(twice(xb, 1), halves(later, 1), NT)
        dbc[b, :, 0:BLK] = (dot(dgram_low, cb, TN) + db_far).astype(BF16)
        dbc[b, :, BLK : 2 * BLK] = (dot(dgram_low, bb) + dc_far).astype(BF16)
        send_out((DX, DBC), b)
        crossing = dot(halves(mix * dmix, 1), strict)
        far_out = jnp.sum(cf * dc_far, axis=1, keepdims=True)
        far_in = jnp.sum(bf * db_far, axis=1, keepdims=True)
        dlog = jnp.sum(jnp.where(causal, crossing + far_out, far_in), axis=0, keepdims=True)
        dlog = dlog + jnp.exp(a_end) * jnp.sum(later * carried)
        direct = jnp.sum(xf * du, axis=1, keepdims=True)
        direct = jnp.sum(jnp.where(same, direct, 0.0), axis=0, keepdims=True)
        dst[b] = jnp.broadcast_to(direct - rate * dlog, (NH, BLK))
        drate = drate - s_row * dlog
        dkeep = dkeep + starts[b : b + 1, :] * dlog
        dskip = dskip + jnp.sum(dy * xf, axis=0, keepdims=True)
        send_out((DST,), b)

    row = lax.broadcasted_iota(jnp.int32, (NH, BLK), 0)
    lane = lax.broadcasted_iota(jnp.int32, (NH, BLK), 1)
    dkeep = jnp.sum(dkeep, axis=1, keepdims=True) / jnp.full((1, 1), keep, F32)
    drate = jnp.sum(drate, axis=1, keepdims=True)
    dskip = jnp.sum(dskip, axis=1, keepdims=True)
    tile = jnp.where(row == 0, drate, jnp.where(row == 1, dkeep, jnp.where(row == 2, dskip, 0.0)))
    tile = jnp.where(lane == z, tile, 0.0)

    def spread(src, buf, place, axis, peers, sems, rsems):
        copies = []
        for i, peer in enumerate(peers):
            copy = pltpu.make_async_remote_copy(
                src_ref=src, dst_ref=buf.at[place],
                send_sem=sems.at[i], recv_sem=rsems.at[place],
                device_id={axis: peer}, device_id_type=MESH,
            )
            copy.start()
            copies.append(copy)
        return copies

    def gathered(buf, place, count, copies, rsems):
        for o in range(1, count):
            source = lax.rem(place + o, count)
            ref = buf.at[source]
            pltpu.make_async_copy(ref, ref, rsems.at[source]).wait()
        for copy in copies:
            copy.wait_send()

    par_x[at_x] = tile
    gathered(par_x, at_x, nx, spread(par_x.at[at_x], par_x, at_x, "dp", x_peers, x_send, x_recv), x_recv)
    par_y[at_y] = jnp.sum(par_x[...], axis=0)
    gathered(par_y, at_y, ny, spread(par_y.at[at_y], par_y, at_y, "dp", y_peers, y_send, y_recv), y_recv)
    par_mine[...] = jnp.sum(par_y[...], axis=0)
    own = pltpu.make_async_copy(par_mine, par_z.at[me], z_recv.at[me])
    own.start()
    z_copies = spread(par_mine, par_z, me, "seq", z_peers, z_send, z_recv)

    for kind in range(6):
        for off in offsets[kind]:
            in_remote(kind, off).wait_send()

    @pl.when(jnp.logical_not(stay))
    def _():
        for kind in range(6):
            in_remote(kind, 0).wait_send()

    for dist, sign, onward in hops:

        @pl.when(from_half(dist, sign))
        def _():
            for j in range(2):
                for kind in onward:
                    hop(kind, dist, sign, j).wait_send()

    outs = (att_got, dqk_got, dx_got, dbc_got, dst_got)
    for c in range(NH):
        for kind in range(5):
            ref = outs[kind].at[0, :, pl.ds(c * BLK, BLK)] if kind in (ATT, DX) else outs[kind].at[c]
            pltpu.make_async_copy(ref, ref, out_recv.at[kind, c]).wait()
    own.wait()
    gathered(par_z, me, 2 * NH, z_copies, z_recv)
    for b in range(NH):

        @pl.when(core * NH + b != me)
        def _():
            for kind in range(5):
                out_remote(kind, b).wait_send()


def epilogue_kernel(
    att_got, dx_got, dqk_got, dbc_got, dst_got, par_z,
    att_out, dq_out, dk_out, dx_out, db_out, dc_out, dstep_out, rate_out, keep_out, skip_out,
):
    att_out[...] = att_got[...]
    dx_out[...] = dx_got[...]
    low = lax.broadcasted_iota(jnp.int32, (BLK, BLK), 1) < 64
    for m in range(NH // 2):
        even, odd = dqk_got[2 * m], dqk_got[2 * m + 1]
        cols = pl.ds(m * BLK, BLK)
        dq_out[0, :, cols] = jnp.where(low, swap_halves(even), odd)
        dk_out[0, :, cols] = jnp.where(low, even, swap_halves(odd))
    total = jnp.zeros((BLK, 2 * BLK), F32)
    for c in range(NH):
        total = total + dbc_got[c].astype(F32)
        dstep_out[0, c : c + 1, :] = dst_got[c, 0:1, :]
    db_out[0] = total[:, 0:BLK].astype(BF16)
    dc_out[0] = total[:, BLK : 2 * BLK].astype(BF16)
    sums = jnp.sum(par_z[...], axis=0)
    rate_out[...] = sums[0:1, 0:NH]
    keep_out[...] = sums[1:2, 0:NH]
    skip_out[...] = sums[2:3, 0:NH]


VM = pl.BlockSpec(memory_space=pltpu.VMEM)
SM = pl.BlockSpec(memory_space=pltpu.SMEM)
ANY = pl.BlockSpec(memory_space=pl.ANY)


def per_device(
    nx, ny, x, b_in, c_out, step, rate, keep, skip, lengths, q, k, lists, go
):
    def arr(*shape, dtype=BF16):
        return jax.ShapeDtypeStruct(shape, dtype)

    def vm(*shape, dtype=BF16):
        return pltpu.VMEM(shape, dtype)

    sq = (BLK, BLK)
    dma = pltpu.SemaphoreType.DMA
    parts = pl.pallas_call(
        partial(main_kernel, nx, ny),
        out_shape=(
            arr(1, BLK, NH * BLK), arr(1, BLK, NH * BLK), arr(NH, *sq), arr(NH, BLK, 2 * BLK),
            arr(NH, NH, BLK, dtype=F32), arr(2 * NH, NH, BLK, dtype=F32),
        ),
        in_specs=[SM] * 5 + [ANY] * 4 + [VM] * 2 + [ANY],
        out_specs=(ANY,) * 6,
        scratch_shapes=[
            vm(NH, *sq), vm(NH, *sq), vm(NH, *sq), vm(NH, *sq), vm(NH, NH, BLK, dtype=F32),
            vm(2 * NH, *sq), vm(NH, *sq), vm(2 * NH, *sq),
            vm(NH, *sq, dtype=F32), vm(NH, *sq, dtype=F32), vm(NH, *sq, dtype=F32),
            vm(NH, *sq, dtype=F32),
            vm(*sq, dtype=F32), vm(*sq, dtype=F32), vm(NH, *sq), vm(NH, *sq),
            vm(LISTED * NH, *sq, dtype=F32), vm(LISTED * NH, *sq, dtype=F32),
            vm(NH, *sq, dtype=F32), vm(NH, *sq, dtype=F32), vm(NH, *sq, dtype=F32),
            vm(NH, *sq, dtype=F32), vm(NH, *sq), vm(NH, *sq),
            vm(NH, *sq, dtype=F32), vm(NH, *sq), vm(NH, *sq), vm(NH, BLK, 2 * BLK),
            vm(NH, NH, BLK, dtype=F32),
            vm(nx, NH, BLK, dtype=F32), vm(ny, NH, BLK, dtype=F32), vm(NH, BLK, dtype=F32),
            dma((6, NH)), dma((6, NH)), dma((2, 6, 2)), dma((6,)), dma((6,)),
            dma((5, NH)), dma((5, NH)),
            dma((nx,)), dma((nx,)), dma((ny,)), dma((ny,)), dma((2 * NH,)), dma((2 * NH,)),
        ],
        compiler_params=pltpu.CompilerParams(collective_id=0, has_side_effects=True),
        name="mixer_attention",
    )(rate, keep, skip, lengths, lists, x, b_in, c_out, step, q, k, go)
    att, dq, dk, dx, db, dc, dstep, drate, dkeep, dskip = pl.pallas_call(
        epilogue_kernel,
        out_shape=(
            arr(1, BLK, NH * BLK), arr(1, BLK, NH * 64), arr(1, BLK, NH * 64),
            arr(1, BLK, NH * BLK), arr(1, *sq), arr(1, *sq), arr(1, NH, BLK, dtype=F32),
            arr(1, NH, dtype=F32), arr(1, NH, dtype=F32), arr(1, NH, dtype=F32),
        ),
        in_specs=[VM] * 6,
        out_specs=(VM,) * 10,
        name="epilogue",
    )(*parts)
    return att, dq, dk, dx, db, dc, dstep, drate.reshape(NH), dkeep.reshape(NH), dskip.reshape(NH)


def solution(mesh):
    rows = P("dp", "seq", None)
    heads = P("dp", None, "seq")
    scene = P("dp", None)
    in_specs = (
        rows, rows, rows, heads, P(), P(), P(), scene, rows, rows, P("dp", None, None), rows,
    )
    out_specs = (rows,) * 6 + (heads, P(), P(), P())
    nx = 4 if mesh.shape["dp"] % 4 == 0 else 1
    ny = mesh.shape["dp"] // nx
    return jax.shard_map(
        partial(per_device, nx, ny), mesh=mesh, in_specs=in_specs, out_specs=out_specs,
        check_vma=False,
    )
```

```python
from functools import partial

import jax
import jax.numpy as jnp
from jax import lax
from jax.experimental import pallas as pl
from jax.experimental.pallas import tpu as pltpu
from jax.sharding import PartitionSpec as P


BLK = 128
NH = 8
LISTED = 4
F32 = jnp.float32
BF16 = jnp.bfloat16
MESH = pl.DeviceIdType.MESH
HIGHEST = lax.Precision.HIGHEST

NN = (((1,), (0,)), ((), ()))
NT = (((1,), (1,)), ((), ()))
TN = (((0,), (0,)), ((), ()))

X, B, C, STEP, QK, GO = range(6)
ATT, DQK, DX, DST = range(4)


def dot(a, b, dims=NN, precision=None):
    return lax.dot_general(a, b, dims, precision=precision, preferred_element_type=F32)


def halves(a, axis):
    high = a.astype(BF16)
    return jnp.concatenate([high, (a - high.astype(F32)).astype(BF16)], axis=axis)


def twice(a, axis):
    return jnp.concatenate([a, a], axis=axis)


def thirds(a, b, axis):
    a_high, b_high = a.astype(BF16), b.astype(BF16)
    a_rest = (a - a_high.astype(F32)).astype(BF16)
    b_rest = (b - b_high.astype(F32)).astype(BF16)
    return (
        jnp.concatenate([a_high, a_rest, a_high], axis=axis),
        jnp.concatenate([b_high, b_high, b_rest], axis=axis),
    )


def tri(kind):
    row = lax.broadcasted_iota(jnp.int32, (BLK, BLK), 0)
    col = lax.broadcasted_iota(jnp.int32, (BLK, BLK), 1)
    return kind(row, col)


def swap_halves(tile):
    return pltpu.roll(tile.astype(F32), 64, 1).astype(tile.dtype)


def decay_parts(step_tiles, z, core, rate, keep, lengths_ref):
    head = lax.broadcasted_iota(jnp.int32, (NH, NH, BLK), 1)
    step = jnp.sum(jnp.where(head == z, step_tiles, 0.0), axis=1)
    chunk = lax.broadcasted_iota(jnp.int32, (NH, BLK), 0)
    lane = lax.broadcasted_iota(jnp.int32, (NH, BLK), 1)
    place = core * (NH * BLK) + chunk * BLK + lane
    starts = jnp.zeros((NH, BLK), F32)
    bound = jnp.int32(0)
    for v in range(lengths_ref.shape[1] - 1):
        bound = bound + lengths_ref[0, v]
        starts = starts + jnp.where(place == bound, 1.0, 0.0)
    log_keep = jnp.log(jnp.full((NH, BLK), keep, F32))
    logs = starts * log_keep - rate * step
    upper = tri(lambda r, c: jnp.where(r <= c, 1.0, 0.0))
    lower = tri(lambda r, c: jnp.where(r >= c, 1.0, 0.0))
    eye = tri(lambda r, c: jnp.where(r == c, 1.0, 0.0))
    cum_row = dot(logs, upper, NN, HIGHEST)
    cum_col = dot(lower, logs, NT, HIGHEST)
    step_col = dot(eye, step, NT, HIGHEST)
    return step, starts, step_col, cum_row, cum_col


def main_kernel(
    nx, ny,
    rate_ref, keep_ref, skip_ref, lengths_ref, lists_ref,
    x_ref, b_ref, c_ref, step_ref, q_ref, k_ref, go_ref,
    att_got, dx_got, dqk_got, dbc_got, dst_got, par_z,
    q_here, k_here, pack, xs, bs, cs, steps, qks, gos, vs, states, fades, mixes, part,
    sent, got, att, dqs, high, dv_parts, dk_parts, dv, dv_out, dv_in, dk, dk_out, dk_in,
    chain, dqk, dx, dbc, folds, whole, dst, par_x, par_y, par_mine,
    load_sem, in_send, in_recv, hop_send, pair_send, pair_recv, block_send, block_recv, fold_send, fold_recv, last_send, last_recv, out_send, out_recv,
    x_send, x_recv, y_send, y_recv, z_send, z_recv,
):
    me = lax.axis_index("seq")
    z, core = me // 2, lax.rem(me, 2)
    hold_half, hold_slot = me // NH, lax.rem(me, NH)
    partner = me + 1 - 2 * core
    dp = lax.axis_index("dp")
    at_x, at_y = lax.rem(dp, nx), dp // nx
    x_peers = [at_y * nx + lax.rem(at_x + o, nx) for o in range(1, nx)]
    y_peers = [lax.rem(at_y + o, ny) * nx + at_x for o in range(1, ny)]
    z_peers = [lax.rem(me + o, 2 * NH) for o in range(1, 2 * NH)]

    barrier = pltpu.get_barrier_semaphore()
    greeted = [{"seq": peer} for peer in z_peers] + [{"dp": peer} for peer in x_peers + y_peers]
    for target in greeted:
        pl.semaphore_signal(barrier, inc=1, device_id=target, device_id_type=MESH)
    loads = [
        pltpu.make_async_copy(src.at[0], dst_ref, load_sem.at[i])
        for i, (src, dst_ref) in enumerate(((q_ref, q_here), (k_ref, k_here)))
    ]
    for load in loads:
        load.start()
    for load in loads:
        load.wait()
    tile_lane = lax.broadcasted_iota(jnp.int32, (BLK, BLK), 1)
    low = tile_lane < 64
    for m in range(NH // 2):
        cols = pl.ds(m * BLK, BLK)
        q_tile, k_tile = q_here[:, cols], k_here[:, cols]
        pack[2 * m] = jnp.where(low, q_tile, swap_halves(k_tile))
        pack[2 * m + 1] = jnp.where(low, swap_halves(q_tile), k_tile)
    pl.semaphore_wait(barrier, len(greeted))

    ins = (xs, bs, cs, steps, qks, gos)

    def in_piece(kind, c):
        cols = pl.ds(pl.multiple_of(c * BLK, BLK), BLK)
        return (
            (x_ref.at[0, :, cols], xs.at[hold_slot]),
            (b_ref.at[0], bs.at[hold_slot]),
            (c_ref.at[0], cs.at[hold_slot]),
            (step_ref.at[0], steps.at[hold_slot]),
            (pack.at[c], qks.at[me]),
            (go_ref.at[0, :, cols], gos.at[hold_slot]),
        )[kind]

    def in_remote(kind, off):
        c = lax.rem(z + off, NH)
        src, dst_ref = in_piece(kind, c)
        return pltpu.make_async_remote_copy(
            src_ref=src, dst_ref=dst_ref,
            send_sem=in_send.at[kind, off], recv_sem=in_recv.at[kind, hold_slot],
            device_id={"seq": 2 * c + hold_half}, device_id_type=MESH,
        )

    stay = hold_half == core
    offsets = {kind: (4, 3, 5, 2, 6, 1, 7) for kind in range(6)}
    offsets[B] = offsets[C] = (1, 7)

    def send_in(kinds, offs):
        for off in offs:
            for kind in kinds:
                in_remote(kind, off).start()

    def keep_in(kinds):
        @pl.when(stay)
        def _():
            for kind in kinds:
                src, dst_ref = in_piece(kind, z)
                pltpu.make_async_copy(src, dst_ref, in_recv.at[kind, hold_slot]).start()

        @pl.when(jnp.logical_not(stay))
        def _():
            for kind in kinds:
                in_remote(kind, 0).start()

    def came(kind, slot):
        ref = ins[kind].at[core * NH + slot] if kind == QK else ins[kind].at[slot]
        pltpu.make_async_copy(ref, ref, in_recv.at[kind, slot]).wait()

    def hop(kind, dist, sign, j):
        source = lax.rem(z - sign * dist + NH, NH)
        slot = 2 * lax.rem(source, NH // 2) + j
        ref = ins[kind].at[slot]
        return pltpu.make_async_remote_copy(
            src_ref=ref, dst_ref=ref,
            send_sem=hop_send.at[kind - B, (dist - 1) * 2 + (1 - sign) // 2, j],
            recv_sem=in_recv.at[kind, slot],
            device_id={"seq": lax.rem(me + 2 * sign + 2 * NH, 2 * NH)}, device_id_type=MESH,
        )

    hops = [
        (dist, sign, [k for k, reach in ((B, 4 if sign > 0 else 3), (C, 3 if sign > 0 else 4))
                      if dist < reach])
        for dist in (1, 2, 3) for sign in (1, -1)
    ]

    def from_half(dist, sign):
        return lax.rem(z - sign * dist + NH, NH) // (NH // 2) == core

    send_in((B, C), (1, 7))
    send_in((X, STEP), (4, 3, 5, 2, 6))
    keep_in(range(6))
    bulk = {1: ((X, STEP), (1, 7), (QK,), (4, 3, 5)), 2: ((QK,), (2, 6, 1, 7), (GO,), (4,)),
            3: ((GO,), (3, 5, 2, 6), (GO,), (1, 7))}
    for dist, sign, onward in hops:

        @pl.when(from_half(dist, sign))
        def _():
            source = lax.rem(z - sign * dist + NH, NH)
            for j in range(2):
                for kind in (B, C):
                    came(kind, 2 * lax.rem(source, NH // 2) + j)
                    if kind in onward:
                        hop(kind, dist, sign, j).start()

        if sign < 0:
            send_in(*bulk[dist][:2])
            send_in(*bulk[dist][2:])

    for dist in (0, 4):

        @pl.when(from_half(dist, 1))
        def _():
            source = lax.rem(z + dist, NH)
            for j in range(2):
                for kind in (B, C):
                    came(kind, 2 * lax.rem(source, NH // 2) + j)

    for slot in range(NH):
        came(X, slot)
        came(STEP, slot)

    rate, keep, skip = rate_ref[z], keep_ref[z], skip_ref[z]
    step, starts, step_col, cum_row, cum_col = decay_parts(
        steps[...], z, core, rate, keep, lengths_ref
    )
    causal = tri(lambda r, c: r >= c)

    def chunk_decay(b):
        a_col, a_row = cum_col[:, b : b + 1], cum_row[b : b + 1, :]
        return a_col, a_row, cum_row[b : b + 1, BLK - 1 : BLK]

    state = jnp.zeros((BLK, BLK), F32)
    for b in range(NH):
        xb, bb, cb = xs[b], bs[b], cs[b]
        a_col, a_row, a_end = chunk_decay(b)
        xf = xb.astype(F32)
        weight = jnp.exp(jnp.minimum(a_end - a_col, 0.0)) * step_col[:, b : b + 1]
        states[b] = state
        state = jnp.exp(a_end) * state + dot(twice(bb, 0), halves(xf * weight, 0), TN)
    sent[...] = state

    def pair(src, dst_ref, i):
        return pltpu.make_async_remote_copy(
            src_ref=src, dst_ref=dst_ref, send_sem=pair_send.at[i], recv_sem=pair_recv.at[i],
            device_id={"seq": partner}, device_id_type=MESH,
        )

    state_copy = pair(sent, got, 0)
    state_copy.start()
    for b in range(NH):
        xb, bb, cb = xs[b], bs[b], cs[b]
        a_col, a_row, a_end = chunk_decay(b)
        fade = jnp.where(causal, jnp.exp(jnp.minimum(a_col - a_row, 0.0)), 0.0)
        fades[b] = fade
        mix = fade * dot(cb, bb, NT)
        mixes[b] = mix
        part[b] = dot((mix * step[b : b + 1, :]).astype(BF16), xb) + skip * xb.astype(F32)
    state_copy.wait()
    entering = got[...] * jnp.where(core == 1, 1.0, 0.0)
    before = jnp.zeros((1, 1), F32)
    for b in range(NH):
        a_col, a_row, a_end = chunk_decay(b)
        carried = states[b] + jnp.exp(before) * entering
        states[b] = carried
        value = part[b] + jnp.exp(a_col) * dot(cs[b], carried.astype(BF16))
        vs[core * NH + b] = value.astype(BF16)
        before = before + a_end

    mine = pl.ds(pl.multiple_of(core * NH, NH), NH)
    value_copy = pair(vs.at[mine], vs.at[mine], 1)
    value_copy.start()

    def pair_block(src, dst_ref, kind, b):
        return pltpu.make_async_remote_copy(
            src_ref=src, dst_ref=dst_ref,
            send_sem=block_send.at[kind, b], recv_sem=block_recv.at[kind, b],
            device_id={"seq": partner}, device_id_type=MESH,
        )

    key_copies = []
    for slot in range(NH):
        came(QK, slot)
        ref = qks.at[core * NH + slot]
        key_copies.append(pair_block(ref, ref, 0, slot))
        key_copies[slot].start()
    value_copy.wait()
    for copy in key_copies:
        copy.wait()

    head_cols = pl.ds(pl.multiple_of(z * BLK, BLK), BLK)

    def out_piece(kind, b):
        return (
            (att.at[b], att_got.at[0, :, head_cols]),
            (dqk.at[b], dqk_got.at[z]),
            (dx.at[b], dx_got.at[0, :, head_cols]),
            (dst.at[b], dst_got.at[z]),
        )[kind]

    def out_remote(kind, b):
        src, dst_ref = out_piece(kind, b)
        return pltpu.make_async_remote_copy(
            src_ref=src, dst_ref=dst_ref,
            send_sem=out_send.at[kind, b], recv_sem=out_recv.at[kind, z],
            device_id={"seq": core * NH + b}, device_id_type=MESH,
        )

    def send_out(kinds, b):
        here = core * NH + b == me

        @pl.when(here)
        def _():
            for kind in kinds:
                src, dst_ref = out_piece(kind, b)
                pltpu.make_async_copy(src, dst_ref, out_recv.at[kind, z]).start()

        @pl.when(jnp.logical_not(here))
        def _():
            for kind in kinds:
                out_remote(kind, b).start()

    zero = jnp.zeros((BLK, BLK), BF16)

    def listed(b):
        return [lists_ref[0, i, core * NH + b] for i in range(LISTED)]

    def listed_keys(b):
        return jnp.concatenate([jnp.where(low, zero, qks[j]) for j in listed(b)], axis=0)

    def listed_values(b):
        return jnp.concatenate([vs[j] for j in listed(b)], axis=0)

    def weigh(b, carry):
        q_high = (pltpu.roll(qks[core * NH + b].astype(F32), 64, 1) * 0.125).astype(BF16)
        scores = dot(listed_keys(b), q_high, NT)
        top = jnp.max(scores, axis=0, keepdims=True)
        weights = jnp.exp(scores - top)
        weights = weights * (1.0 / jnp.sum(weights, axis=0, keepdims=True))
        high[b] = weights
        att[b] = dot(weights.astype(BF16), listed_values(b), TN).astype(BF16)
        send_out((ATT,), b)
        return carry

    def value_grads(b, carry):
        came(GO, b)
        dv_parts[pl.ds(b * LISTED, LISTED)] = dot(high[b].astype(BF16), gos[b]).reshape(
            LISTED, BLK, BLK
        )
        return carry

    def score_grads(b, carry):
        weights = high[b]
        dweights = dot(listed_values(b), gos[b], NT)
        delta = jnp.sum(weights * dweights, axis=0, keepdims=True)
        dscores = (weights * (dweights - delta) * 0.125).astype(BF16)
        dqs[b] = dot(dscores, listed_keys(b), TN).astype(BF16)
        q_low = jnp.where(low, qks[core * NH + b], zero)
        dk_parts[pl.ds(b * LISTED, LISTED)] = dot(dscores, q_low).reshape(LISTED, BLK, BLK)
        return carry

    def key_sum(parts, j):
        total = jnp.zeros((BLK, BLK), F32)
        for b in range(NH):
            slot = jnp.int32(0)
            lists = jnp.int32(0)
            for i in range(LISTED):
                hit = (lists_ref[0, i, core * NH + b] == j).astype(jnp.int32)
                slot = slot + i * hit
                lists = lists + hit
            slot = jnp.minimum(slot, LISTED - 1)
            total = total + lists.astype(F32) * parts[b * LISTED + slot]
        return total

    def dv_copy(j):
        return pair_block(dv_out.at[j], dv_in.at[j], 1, j)

    def dv_for_partner(i, carry):
        j = NH - 1 - i
        dv_out[j] = key_sum(dv_parts, (1 - core) * NH + j)
        dv_copy(j).start()
        return carry

    def dv_for_me(j, carry):
        dv[j] = key_sum(dv_parts, core * NH + j)
        return carry

    def dk_for_partner(j, carry):
        dk_out[j] = key_sum(dk_parts, (1 - core) * NH + j).astype(BF16)
        return carry

    def dk_for_me(j, carry):
        dk[j] = key_sum(dk_parts, core * NH + j)
        return carry

    lax.fori_loop(0, NH, weigh, 0)
    lax.fori_loop(0, NH, value_grads, 0)
    lax.fori_loop(0, NH, dv_for_partner, 0)
    lax.fori_loop(0, NH, dv_for_me, 0)

    tail = jnp.zeros((BLK, BLK), F32)
    for b in reversed(range(NH)):
        a_col, a_row, a_end = chunk_decay(b)
        dv_copy(b).wait()
        dy = dv[b] + dv_in[b]
        dv[b] = dy
        chain[b] = tail
        tail = jnp.exp(a_end) * tail + dot(twice(cs[b], 0), halves(dy * jnp.exp(a_col), 0), TN)
    sent[...] = tail
    tail_copy = pair(sent, got, 5)
    tail_copy.start()
    lax.fori_loop(0, NH // 2, score_grads, 0)
    tail_copy.wait()
    leaving = got[...] * jnp.where(core == 0, 1.0, 0.0)

    same = tri(lambda r, c: r == c)
    strict = twice(tri(lambda r, c: jnp.where(r < c, 1.0, 0.0)).astype(BF16), 0)
    after = jnp.zeros((1, 1), F32)
    drate = jnp.zeros((1, BLK), F32)
    dkeep = jnp.zeros((1, BLK), F32)
    dskip = jnp.zeros((1, BLK), F32)
    for b in reversed(range(NH)):
        xb, bb, cb = xs[b], bs[b], cs[b]
        xf, bf, cf = xb.astype(F32), bb.astype(F32), cb.astype(F32)
        dy = dv[b]
        a_col, a_row, a_end = chunk_decay(b)
        s_col, s_row = step_col[:, b : b + 1], step[b : b + 1, :]
        later = chain[b] + jnp.exp(after) * leaving
        later_low = later.astype(BF16)
        carried = states[b]
        after = after + a_end
        mix = mixes[b]
        dmix = s_row * dot(halves(dy, 1), twice(xb, 1), NT)
        dgram_low = (fades[b] * dmix).astype(BF16)
        to_end = jnp.exp(jnp.minimum(a_end - a_col, 0.0))
        du = dot(mix.astype(BF16), dy.astype(BF16), TN) + to_end * dot(bb, later_low)
        dx[b] = (s_col * du + skip * dy).astype(BF16)
        dc_far = jnp.exp(a_col) * dot(*thirds(dy, carried, 1), NT)
        db_far = to_end * s_col * dot(twice(xb, 1), halves(later, 1), NT)
        dbc[0, b] = (dot(dgram_low, cb, TN) + db_far).astype(BF16)
        dbc[1, b] = (dot(dgram_low, bb) + dc_far).astype(BF16)
        crossing = dot(halves(mix * dmix, 1), strict)
        far_out = jnp.sum(cf * dc_far, axis=1, keepdims=True)
        far_in = jnp.sum(bf * db_far, axis=1, keepdims=True)
        dlog = jnp.sum(jnp.where(causal, crossing + far_out, far_in), axis=0, keepdims=True)
        dlog = dlog + jnp.exp(a_end) * jnp.sum(later * carried)
        direct = jnp.sum(xf * du, axis=1, keepdims=True)
        direct = jnp.sum(jnp.where(same, direct, 0.0), axis=0, keepdims=True)
        dst[b] = jnp.broadcast_to(direct - rate * dlog, (NH, BLK))
        drate = drate - s_row * dlog
        dkeep = dkeep + starts[b : b + 1, :] * dlog
        dskip = dskip + jnp.sum(dy * xf, axis=0, keepdims=True)

    row = lax.broadcasted_iota(jnp.int32, (NH, BLK), 0)
    lane = lax.broadcasted_iota(jnp.int32, (NH, BLK), 1)
    dkeep = jnp.sum(dkeep, axis=1, keepdims=True) / jnp.full((1, 1), keep, F32)
    drate = jnp.sum(drate, axis=1, keepdims=True)
    dskip = jnp.sum(dskip, axis=1, keepdims=True)
    tile = jnp.where(row == 0, drate, jnp.where(row == 1, dkeep, jnp.where(row == 2, dskip, 0.0)))
    tile = jnp.where(lane == z, tile, 0.0)

    def spread(src, buf, place, axis, peers, sems, rsems):
        copies = []
        for i, peer in enumerate(peers):
            copy = pltpu.make_async_remote_copy(
                src_ref=src, dst_ref=buf.at[place],
                send_sem=sems.at[i], recv_sem=rsems.at[place],
                device_id={axis: peer}, device_id_type=MESH,
            )
            copy.start()
            copies.append(copy)
        return copies

    def gathered(buf, place, count, copies, rsems):
        for o in range(1, count):
            source = lax.rem(place + o, count)
            ref = buf.at[source]
            pltpu.make_async_copy(ref, ref, rsems.at[source]).wait()
        for copy in copies:
            copy.wait_send()

    par_x[at_x] = tile

    def fold(kind, up, slot):
        return pltpu.make_async_remote_copy(
            src_ref=folds.at[kind, up, slot], dst_ref=folds.at[kind, up, slot],
            send_sem=fold_send.at[kind, up, slot], recv_sem=fold_recv.at[kind, up, slot],
            device_id={"seq": lax.rem(me + (2 if up else 2 * NH - 2), 2 * NH)},
            device_id_type=MESH,
        )

    def fold_came(kind, up, slot):
        ref = folds.at[kind, up, slot]
        pltpu.make_async_copy(ref, ref, fold_recv.at[kind, up, slot]).wait()

    def fold_place(dist, up):
        holder = lax.rem(z + (dist if up else NH - dist), NH)
        return holder // (NH // 2) == core, lax.rem(holder, NH // 2)

    def fold_kinds(dist, up):
        return [(kind, reach) for kind, reach in ((0, 4 - up), (1, 3 + up)) if dist <= reach]

    def fold_step(dist):
        for up in (0, 1):
            ours, slot = fold_place(dist, up)

            @pl.when(ours)
            def _():
                for kind, reach in fold_kinds(dist, up):
                    own_part = dbc[kind, pl.ds(2 * slot, 2)]
                    if dist < reach:
                        fold_came(kind, up, slot)
                        total = own_part.astype(F32) + folds[kind, up, slot].astype(F32)
                        folds[kind, up, slot] = total.astype(BF16)
                    else:
                        folds[kind, up, slot] = own_part
                    fold(kind, up, slot).start()

    def send_blocks(kinds, first, count):
        for off in range(first, first + count):
            send_out(kinds, lax.rem(hold_slot + off, NH))

    fold_step(4)
    send_blocks((DX, DST), 0, NH // 2)
    x_copies = spread(par_x.at[at_x], par_x, at_x, "dp", x_peers, x_send, x_recv)
    lax.fori_loop(NH // 2, NH, score_grads, 0)
    fold_step(3)
    send_blocks((DX, DST), NH // 2, NH // 2)
    lax.fori_loop(0, NH, dk_for_partner, 0)
    dk_copy = pair(dk_out, dk_in, 4)
    dk_copy.start()
    gathered(par_x, at_x, nx, x_copies, x_recv)
    par_y[at_y] = jnp.sum(par_x[...], axis=0)
    y_copies = spread(par_y.at[at_y], par_y, at_y, "dp", y_peers, y_send, y_recv)
    fold_step(2)
    lax.fori_loop(0, NH, dk_for_me, 0)
    dk_copy.wait()
    for b in range(NH):
        dqk[b] = (dk[b] + dk_in[b].astype(F32) + dqs[b].astype(F32)).astype(BF16)
    send_blocks((DQK,), 0, NH // 2)
    fold_step(1)
    gathered(par_y, at_y, ny, y_copies, y_recv)
    par_mine[...] = jnp.sum(par_y[...], axis=0)
    own = pltpu.make_async_copy(par_mine, par_z.at[me], z_recv.at[me])
    own.start()
    z_copies = spread(par_mine, par_z, me, "seq", z_peers, z_send, z_recv)
    send_blocks((DQK,), NH // 2, NH // 2)
    last_half = z // (NH // 2) == core
    last_slot = lax.rem(z, NH // 2)
    to_me = pltpu.make_async_copy(whole.at[core], dbc_got, last_recv.at[0])
    to_partner = pltpu.make_async_remote_copy(
        src_ref=whole.at[1 - core], dst_ref=dbc_got, send_sem=last_send.at[0],
        recv_sem=last_recv.at[0], device_id={"seq": partner}, device_id_type=MESH,
    )

    @pl.when(last_half)
    def _():
        for kind in range(2):
            fold_came(kind, 0, last_slot)
            fold_came(kind, 1, last_slot)
            total = dbc[kind, pl.ds(2 * last_slot, 2)].astype(F32)
            total = total + folds[kind, 0, last_slot].astype(F32)
            total = (total + folds[kind, 1, last_slot].astype(F32)).astype(BF16)
            whole[0, kind] = total[0]
            whole[1, kind] = total[1]
        to_partner.start()
        to_me.start()


    for kind in range(6):
        for off in offsets[kind]:
            in_remote(kind, off).wait_send()

    @pl.when(jnp.logical_not(stay))
    def _():
        for kind in range(6):
            in_remote(kind, 0).wait_send()

    for dist, sign, onward in hops:

        @pl.when(from_half(dist, sign))
        def _():
            for j in range(2):
                for kind in onward:
                    hop(kind, dist, sign, j).wait_send()

    for dist in (4, 3, 2, 1):
        for up in (0, 1):
            ours, slot = fold_place(dist, up)

            @pl.when(ours)
            def _():
                for kind, _ in fold_kinds(dist, up):
                    fold(kind, up, slot).wait_send()

    @pl.when(last_half)
    def _():
        to_partner.wait_send()

    pltpu.make_async_copy(dbc_got, dbc_got, last_recv.at[0]).wait()
    outs = (att_got, dqk_got, dx_got, dst_got)
    for c in range(NH):
        for kind in range(4):
            ref = outs[kind].at[0, :, pl.ds(c * BLK, BLK)] if kind in (ATT, DX) else outs[kind].at[c]
            pltpu.make_async_copy(ref, ref, out_recv.at[kind, c]).wait()
    own.wait()
    gathered(par_z, me, 2 * NH, z_copies, z_recv)
    for b in range(NH):

        @pl.when(core * NH + b != me)
        def _():
            for kind in range(4):
                out_remote(kind, b).wait_send()


def epilogue_kernel(
    att_got, dx_got, dqk_got, dbc_got, dst_got, par_z,
    att_out, dq_out, dk_out, dx_out, db_out, dc_out, dstep_out, rate_out, keep_out, skip_out,
):
    att_out[...] = att_got[...]
    dx_out[...] = dx_got[...]
    low = lax.broadcasted_iota(jnp.int32, (BLK, BLK), 1) < 64
    for m in range(NH // 2):
        even, odd = dqk_got[2 * m], dqk_got[2 * m + 1]
        cols = pl.ds(m * BLK, BLK)
        dq_out[0, :, cols] = jnp.where(low, swap_halves(even), odd)
        dk_out[0, :, cols] = jnp.where(low, even, swap_halves(odd))
    for c in range(NH):
        dstep_out[0, c : c + 1, :] = dst_got[c, 0:1, :]
    db_out[0] = dbc_got[0]
    dc_out[0] = dbc_got[1]
    sums = jnp.sum(par_z[...], axis=0)
    rate_out[...] = sums[0:1, 0:NH]
    keep_out[...] = sums[1:2, 0:NH]
    skip_out[...] = sums[2:3, 0:NH]


VM = pl.BlockSpec(memory_space=pltpu.VMEM)
SM = pl.BlockSpec(memory_space=pltpu.SMEM)
ANY = pl.BlockSpec(memory_space=pl.ANY)


def per_device(
    nx, ny, x, b_in, c_out, step, rate, keep, skip, lengths, q, k, lists, go
):
    def arr(*shape, dtype=BF16):
        return jax.ShapeDtypeStruct(shape, dtype)

    def vm(*shape, dtype=BF16):
        return pltpu.VMEM(shape, dtype)

    sq = (BLK, BLK)
    dma = pltpu.SemaphoreType.DMA
    parts = pl.pallas_call(
        partial(main_kernel, nx, ny),
        out_shape=(
            arr(1, BLK, NH * BLK), arr(1, BLK, NH * BLK), arr(NH, *sq), arr(2, *sq),
            arr(NH, NH, BLK, dtype=F32), arr(2 * NH, NH, BLK, dtype=F32),
        ),
        in_specs=[SM] * 5 + [ANY] * 7,
        out_specs=(ANY,) * 6,
        scratch_shapes=[
            vm(BLK, NH * 64), vm(BLK, NH * 64), vm(NH, *sq),
            vm(NH, *sq), vm(NH, *sq), vm(NH, *sq), vm(NH, NH, BLK, dtype=F32),
            vm(2 * NH, *sq), vm(NH, *sq), vm(2 * NH, *sq),
            vm(NH, *sq, dtype=F32), vm(NH, *sq, dtype=F32), vm(NH, *sq, dtype=F32),
            vm(NH, *sq, dtype=F32),
            vm(*sq, dtype=F32), vm(*sq, dtype=F32), vm(NH, *sq), vm(NH, *sq),
            vm(NH, LISTED * BLK, BLK, dtype=F32),
            vm(LISTED * NH, *sq, dtype=F32), vm(LISTED * NH, *sq, dtype=F32),
            vm(NH, *sq, dtype=F32), vm(NH, *sq, dtype=F32), vm(NH, *sq, dtype=F32),
            vm(NH, *sq, dtype=F32), vm(NH, *sq), vm(NH, *sq),
            vm(NH, *sq, dtype=F32), vm(NH, *sq), vm(NH, *sq), vm(2, NH, *sq),
            vm(2, 2, NH // 2, 2, *sq), vm(2, 2, *sq),
            vm(NH, NH, BLK, dtype=F32),
            vm(nx, NH, BLK, dtype=F32), vm(ny, NH, BLK, dtype=F32), vm(NH, BLK, dtype=F32),
            dma((2,)), dma((6, NH)), dma((6, NH)), dma((2, 6, 2)), dma((6,)), dma((6,)), dma((2, NH)), dma((2, NH)),
            dma((2, 2, NH // 2)), dma((2, 2, NH // 2)), dma((1,)), dma((1,)),
            dma((4, NH)), dma((4, NH)),
            dma((nx,)), dma((nx,)), dma((ny,)), dma((ny,)), dma((2 * NH,)), dma((2 * NH,)),
        ],
        compiler_params=pltpu.CompilerParams(collective_id=0, has_side_effects=True),
        name="mixer_attention",
    )(rate, keep, skip, lengths, jnp.transpose(lists, (0, 2, 1)), x, b_in, c_out, step, q, k, go)
    att, dq, dk, dx, db, dc, dstep, drate, dkeep, dskip = pl.pallas_call(
        epilogue_kernel,
        out_shape=(
            arr(1, BLK, NH * BLK), arr(1, BLK, NH * 64), arr(1, BLK, NH * 64),
            arr(1, BLK, NH * BLK), arr(1, *sq), arr(1, *sq), arr(1, NH, BLK, dtype=F32),
            arr(1, NH, dtype=F32), arr(1, NH, dtype=F32), arr(1, NH, dtype=F32),
        ),
        in_specs=[VM] * 6,
        out_specs=(VM,) * 10,
        name="epilogue",
    )(*parts)
    return att, dq, dk, dx, db, dc, dstep, drate.reshape(NH), dkeep.reshape(NH), dskip.reshape(NH)


def solution(mesh):
    rows = P("dp", "seq", None)
    heads = P("dp", None, "seq")
    scene = P("dp", None)
    in_specs = (
        rows, rows, rows, heads, P(), P(), P(), scene, rows, rows, P("dp", None, None), rows,
    )
    out_specs = (rows,) * 6 + (heads, P(), P(), P())
    nx = 4 if mesh.shape["dp"] % 4 == 0 else 1
    ny = mesh.shape["dp"] // nx
    return jax.shard_map(
        partial(per_device, nx, ny), mesh=mesh, in_specs=in_specs, out_specs=out_specs,
        check_vma=False,
    )
```

```python
from functools import partial

import jax
import jax.numpy as jnp
from jax import lax
from jax.experimental import pallas as pl
from jax.experimental.pallas import tpu as pltpu
from jax.sharding import PartitionSpec as P


BLK = 128
NH = 8
LISTED = 4
F32 = jnp.float32
BF16 = jnp.bfloat16
MESH = pl.DeviceIdType.MESH
HIGHEST = lax.Precision.HIGHEST

NN = (((1,), (0,)), ((), ()))
NT = (((1,), (1,)), ((), ()))
TN = (((0,), (0,)), ((), ()))

X, B, C, STEP, QK, GO = range(6)
ATT, DQK, DX, DST = range(4)


def dot(a, b, dims=NN, precision=None):
    return lax.dot_general(a, b, dims, precision=precision, preferred_element_type=F32)


def halves(a, axis):
    high = a.astype(BF16)
    return jnp.concatenate([high, (a - high.astype(F32)).astype(BF16)], axis=axis)


def twice(a, axis):
    return jnp.concatenate([a, a], axis=axis)


def thirds(a, b, axis):
    a_high, b_high = a.astype(BF16), b.astype(BF16)
    a_rest = (a - a_high.astype(F32)).astype(BF16)
    b_rest = (b - b_high.astype(F32)).astype(BF16)
    return (
        jnp.concatenate([a_high, a_rest, a_high], axis=axis),
        jnp.concatenate([b_high, b_high, b_rest], axis=axis),
    )


def tri(kind):
    row = lax.broadcasted_iota(jnp.int32, (BLK, BLK), 0)
    col = lax.broadcasted_iota(jnp.int32, (BLK, BLK), 1)
    return kind(row, col)


def swap_halves(tile):
    return pltpu.roll(tile.astype(F32), 64, 1).astype(tile.dtype)


def decay_parts(step_tiles, z, core, rate, keep, lengths_ref):
    head = lax.broadcasted_iota(jnp.int32, (NH, NH, BLK), 1)
    step = jnp.sum(jnp.where(head == z, step_tiles, 0.0), axis=1)
    chunk = lax.broadcasted_iota(jnp.int32, (NH, BLK), 0)
    lane = lax.broadcasted_iota(jnp.int32, (NH, BLK), 1)
    place = core * (NH * BLK) + chunk * BLK + lane
    starts = jnp.zeros((NH, BLK), F32)
    bound = jnp.int32(0)
    for v in range(lengths_ref.shape[1] - 1):
        bound = bound + lengths_ref[0, v]
        starts = starts + jnp.where(place == bound, 1.0, 0.0)
    log_keep = jnp.log(jnp.full((NH, BLK), keep, F32))
    logs = starts * log_keep - rate * step
    upper = tri(lambda r, c: jnp.where(r <= c, 1.0, 0.0))
    lower = tri(lambda r, c: jnp.where(r >= c, 1.0, 0.0))
    eye = tri(lambda r, c: jnp.where(r == c, 1.0, 0.0))
    cum_row = dot(logs, upper, NN, HIGHEST)
    cum_col = dot(lower, logs, NT, HIGHEST)
    step_col = dot(eye, step, NT, HIGHEST)
    return step, starts, step_col, cum_row, cum_col


def main_kernel(
    nx, ny,
    rate_ref, keep_ref, skip_ref, lengths_ref, lists_ref,
    x_ref, b_ref, c_ref, step_ref, q_ref, k_ref, go_ref,
    att_got, dx_got, dqk_got, dbc_got, dst_got, par_z,
    q_here, k_here, pack, xs, bs, cs, steps, qks, gos, vs, states, fades, mixes, part,
    sent, got, att, dqs, high, dv_parts, dk_parts, dv, dv_out, dv_in, dk, dk_out, dk_in,
    chain, dqk, dx, dbc, folds, whole, dst, par_x, par_y, par_mine,
    load_sem, in_send, in_recv, hop_send, pair_send, pair_recv, block_send, block_recv, fold_send, fold_recv, last_send, last_recv, out_send, out_recv,
    x_send, x_recv, y_send, y_recv, z_send, z_recv,
):
    me = lax.axis_index("seq")
    z, core = me // 2, lax.rem(me, 2)
    hold_half, hold_slot = me // NH, lax.rem(me, NH)
    partner = me + 1 - 2 * core
    dp = lax.axis_index("dp")
    at_x, at_y = lax.rem(dp, nx), dp // nx
    x_peers = [at_y * nx + lax.rem(at_x + o, nx) for o in range(1, nx)]
    y_peers = [lax.rem(at_y + o, ny) * nx + at_x for o in range(1, ny)]
    z_peers = [lax.rem(me + o, 2 * NH) for o in range(1, 2 * NH)]

    barrier = pltpu.get_barrier_semaphore()
    greeted = [{"seq": peer} for peer in z_peers] + [{"dp": peer} for peer in x_peers + y_peers]
    for target in greeted:
        pl.semaphore_signal(barrier, inc=1, device_id=target, device_id_type=MESH)
    loads = [
        pltpu.make_async_copy(src.at[0], dst_ref, load_sem.at[i])
        for i, (src, dst_ref) in enumerate(((q_ref, q_here), (k_ref, k_here)))
    ]
    for load in loads:
        load.start()
    for load in loads:
        load.wait()
    tile_lane = lax.broadcasted_iota(jnp.int32, (BLK, BLK), 1)
    low = tile_lane < 64
    for m in range(NH // 2):
        cols = pl.ds(m * BLK, BLK)
        q_tile, k_tile = q_here[:, cols], k_here[:, cols]
        pack[2 * m] = jnp.where(low, q_tile, swap_halves(k_tile))
        pack[2 * m + 1] = jnp.where(low, swap_halves(q_tile), k_tile)
    pl.semaphore_wait(barrier, len(greeted))

    ins = (xs, bs, cs, steps, qks, gos)

    def in_piece(kind, c):
        cols = pl.ds(pl.multiple_of(c * BLK, BLK), BLK)
        return (
            (x_ref.at[0, :, cols], xs.at[hold_slot]),
            (b_ref.at[0], bs.at[hold_slot]),
            (c_ref.at[0], cs.at[hold_slot]),
            (step_ref.at[0], steps.at[hold_slot]),
            (pack.at[c], qks.at[me]),
            (go_ref.at[0, :, cols], gos.at[hold_slot]),
        )[kind]

    def in_remote(kind, off):
        c = lax.rem(z + off, NH)
        src, dst_ref = in_piece(kind, c)
        return pltpu.make_async_remote_copy(
            src_ref=src, dst_ref=dst_ref,
            send_sem=in_send.at[kind, off], recv_sem=in_recv.at[kind, hold_slot],
            device_id={"seq": 2 * c + hold_half}, device_id_type=MESH,
        )

    stay = hold_half == core
    offsets = {kind: (4, 3, 5, 2, 6, 1, 7) for kind in range(6)}
    offsets[B] = offsets[C] = (1, 7)

    def send_in(kinds, offs):
        for off in offs:
            for kind in kinds:
                in_remote(kind, off).start()

    def keep_in(kinds):
        @pl.when(stay)
        def _():
            for kind in kinds:
                src, dst_ref = in_piece(kind, z)
                pltpu.make_async_copy(src, dst_ref, in_recv.at[kind, hold_slot]).start()

        @pl.when(jnp.logical_not(stay))
        def _():
            for kind in kinds:
                in_remote(kind, 0).start()

    def came(kind, slot):
        ref = ins[kind].at[core * NH + slot] if kind == QK else ins[kind].at[slot]
        pltpu.make_async_copy(ref, ref, in_recv.at[kind, slot]).wait()

    def hop(kind, dist, sign, j):
        source = lax.rem(z - sign * dist + NH, NH)
        slot = 2 * lax.rem(source, NH // 2) + j
        ref = ins[kind].at[slot]
        return pltpu.make_async_remote_copy(
            src_ref=ref, dst_ref=ref,
            send_sem=hop_send.at[kind - B, (dist - 1) * 2 + (1 - sign) // 2, j],
            recv_sem=in_recv.at[kind, slot],
            device_id={"seq": lax.rem(me + 2 * sign + 2 * NH, 2 * NH)}, device_id_type=MESH,
        )

    hops = [
        (dist, sign, [k for k, reach in ((B, 4 if sign > 0 else 3), (C, 3 if sign > 0 else 4))
                      if dist < reach])
        for dist in (1, 2, 3) for sign in (1, -1)
    ]

    def from_half(dist, sign):
        return lax.rem(z - sign * dist + NH, NH) // (NH // 2) == core

    send_in((B, C), (1, 7))
    send_in((X, STEP), (4, 3, 5, 2, 6))
    keep_in(range(6))
    bulk = {1: ((X, STEP), (1, 7), (QK,), (4, 3, 5)), 2: ((QK,), (2, 6, 1, 7), (GO,), (4,)),
            3: ((GO,), (3, 5, 2, 6), (GO,), (1, 7))}
    for dist, sign, onward in hops:

        @pl.when(from_half(dist, sign))
        def _():
            source = lax.rem(z - sign * dist + NH, NH)
            for j in range(2):
                for kind in (B, C):
                    came(kind, 2 * lax.rem(source, NH // 2) + j)
                    if kind in onward:
                        hop(kind, dist, sign, j).start()

        if sign < 0:
            send_in(*bulk[dist][:2])
            send_in(*bulk[dist][2:])

    for dist in (0, 4):

        @pl.when(from_half(dist, 1))
        def _():
            source = lax.rem(z + dist, NH)
            for j in range(2):
                for kind in (B, C):
                    came(kind, 2 * lax.rem(source, NH // 2) + j)

    for slot in range(NH):
        came(X, slot)
        came(STEP, slot)

    rate, keep, skip = rate_ref[z], keep_ref[z], skip_ref[z]
    step, starts, step_col, cum_row, cum_col = decay_parts(
        steps[...], z, core, rate, keep, lengths_ref
    )
    causal = tri(lambda r, c: r >= c)

    def chunk_decay(b):
        a_col, a_row = cum_col[:, b : b + 1], cum_row[b : b + 1, :]
        return a_col, a_row, cum_row[b : b + 1, BLK - 1 : BLK]

    state = jnp.zeros((BLK, BLK), F32)
    for b in range(NH):
        xb, bb, cb = xs[b], bs[b], cs[b]
        a_col, a_row, a_end = chunk_decay(b)
        xf = xb.astype(F32)
        weight = jnp.exp(jnp.minimum(a_end - a_col, 0.0)) * step_col[:, b : b + 1]
        states[b] = state
        state = jnp.exp(a_end) * state + dot(twice(bb, 0), halves(xf * weight, 0), TN)
    sent[...] = state

    def pair(src, dst_ref, i):
        return pltpu.make_async_remote_copy(
            src_ref=src, dst_ref=dst_ref, send_sem=pair_send.at[i], recv_sem=pair_recv.at[i],
            device_id={"seq": partner}, device_id_type=MESH,
        )

    state_copy = pair(sent, got, 0)
    state_copy.start()
    for b in range(NH):
        xb, bb, cb = xs[b], bs[b], cs[b]
        a_col, a_row, a_end = chunk_decay(b)
        fade = jnp.where(causal, jnp.exp(jnp.minimum(a_col - a_row, 0.0)), 0.0)
        fades[b] = fade
        mix = fade * dot(cb, bb, NT)
        mixes[b] = mix
        part[b] = dot((mix * step[b : b + 1, :]).astype(BF16), xb) + skip * xb.astype(F32)
    state_copy.wait()
    entering = got[...] * jnp.where(core == 1, 1.0, 0.0)
    before = jnp.zeros((1, 1), F32)
    for b in range(NH):
        a_col, a_row, a_end = chunk_decay(b)
        carried = states[b] + jnp.exp(before) * entering
        states[b] = carried
        value = part[b] + jnp.exp(a_col) * dot(cs[b], carried.astype(BF16))
        vs[core * NH + b] = value.astype(BF16)
        before = before + a_end

    mine = pl.ds(pl.multiple_of(core * NH, NH), NH)
    value_copy = pair(vs.at[mine], vs.at[mine], 1)
    value_copy.start()

    def pair_block(src, dst_ref, kind, b):
        return pltpu.make_async_remote_copy(
            src_ref=src, dst_ref=dst_ref,
            send_sem=block_send.at[kind, b], recv_sem=block_recv.at[kind, b],
            device_id={"seq": partner}, device_id_type=MESH,
        )

    key_copies = []
    for slot in range(NH):
        came(QK, slot)
        ref = qks.at[core * NH + slot]
        key_copies.append(pair_block(ref, ref, 0, slot))
        key_copies[slot].start()
    for copy in key_copies:
        copy.wait()

    head_cols = pl.ds(pl.multiple_of(z * BLK, BLK), BLK)

    def out_piece(kind, b):
        return (
            (att.at[b], att_got.at[0, :, head_cols]),
            (dqk.at[b], dqk_got.at[z]),
            (dx.at[b], dx_got.at[0, :, head_cols]),
            (dst.at[b], dst_got.at[z]),
        )[kind]

    def out_remote(kind, b):
        src, dst_ref = out_piece(kind, b)
        return pltpu.make_async_remote_copy(
            src_ref=src, dst_ref=dst_ref,
            send_sem=out_send.at[kind, b], recv_sem=out_recv.at[kind, z],
            device_id={"seq": core * NH + b}, device_id_type=MESH,
        )

    def send_out(kinds, b):
        here = core * NH + b == me

        @pl.when(here)
        def _():
            for kind in kinds:
                src, dst_ref = out_piece(kind, b)
                pltpu.make_async_copy(src, dst_ref, out_recv.at[kind, z]).start()

        @pl.when(jnp.logical_not(here))
        def _():
            for kind in kinds:
                out_remote(kind, b).start()

    zero = jnp.zeros((BLK, BLK), BF16)

    def listed(b):
        return [lists_ref[0, i, core * NH + b] for i in range(LISTED)]

    def listed_keys(b):
        return jnp.concatenate([jnp.where(low, zero, qks[j]) for j in listed(b)], axis=0)

    def listed_values(b):
        return jnp.concatenate([vs[j] for j in listed(b)], axis=0)

    def weigh(b, carry):
        q_high = (pltpu.roll(qks[core * NH + b].astype(F32), 64, 1) * 0.125).astype(BF16)
        scores = dot(listed_keys(b), q_high, NT)
        top = jnp.max(scores, axis=0, keepdims=True)
        weights = jnp.exp(scores - top)
        weights = weights * (1.0 / jnp.sum(weights, axis=0, keepdims=True))
        high[b] = weights
        return carry

    def attend(b, carry):
        att[b] = dot(high[b].astype(BF16), listed_values(b), TN).astype(BF16)
        send_out((ATT,), b)
        return carry

    def value_grads(b, carry):
        came(GO, b)
        dv_parts[pl.ds(b * LISTED, LISTED)] = dot(high[b].astype(BF16), gos[b]).reshape(
            LISTED, BLK, BLK
        )
        return carry

    def score_grads(b, carry):
        weights = high[b]
        dweights = dot(listed_values(b), gos[b], NT)
        delta = jnp.sum(weights * dweights, axis=0, keepdims=True)
        dscores = (weights * (dweights - delta) * 0.125).astype(BF16)
        dqs[b] = dot(dscores, listed_keys(b), TN).astype(BF16)
        q_low = jnp.where(low, qks[core * NH + b], zero)
        dk_parts[pl.ds(b * LISTED, LISTED)] = dot(dscores, q_low).reshape(LISTED, BLK, BLK)
        return carry

    def key_sum(parts, j):
        total = jnp.zeros((BLK, BLK), F32)
        for b in range(NH):
            slot = jnp.int32(0)
            lists = jnp.int32(0)
            for i in range(LISTED):
                hit = (lists_ref[0, i, core * NH + b] == j).astype(jnp.int32)
                slot = slot + i * hit
                lists = lists + hit
            slot = jnp.minimum(slot, LISTED - 1)
            total = total + lists.astype(F32) * parts[b * LISTED + slot]
        return total

    def dv_copy(j):
        return pair_block(dv_out.at[j], dv_in.at[j], 1, j)

    def dv_for_partner(i, carry):
        j = NH - 1 - i
        dv_out[j] = key_sum(dv_parts, (1 - core) * NH + j)
        dv_copy(j).start()
        return carry

    def dv_for_me(j, carry):
        dv[j] = key_sum(dv_parts, core * NH + j)
        return carry

    def dk_for_partner(j, carry):
        dk_out[j] = key_sum(dk_parts, (1 - core) * NH + j).astype(BF16)
        return carry

    def dk_for_me(j, carry):
        dk[j] = key_sum(dk_parts, core * NH + j)
        return carry

    lax.fori_loop(0, NH, weigh, 0)
    lax.fori_loop(0, NH, value_grads, 0)
    lax.fori_loop(0, NH, dv_for_partner, 0)
    lax.fori_loop(0, NH, dv_for_me, 0)
    value_copy.wait()
    lax.fori_loop(0, NH // 2, attend, 0)

    tail = jnp.zeros((BLK, BLK), F32)
    for b in reversed(range(NH)):
        a_col, a_row, a_end = chunk_decay(b)
        dv_copy(b).wait()
        dy = dv[b] + dv_in[b]
        dv[b] = dy
        chain[b] = tail
        tail = jnp.exp(a_end) * tail + dot(twice(cs[b], 0), halves(dy * jnp.exp(a_col), 0), TN)
    sent[...] = tail
    tail_copy = pair(sent, got, 5)
    tail_copy.start()
    lax.fori_loop(NH // 2, NH, attend, 0)
    lax.fori_loop(0, 1, score_grads, 0)
    tail_copy.wait()
    leaving = got[...] * jnp.where(core == 0, 1.0, 0.0)

    same = tri(lambda r, c: r == c)
    strict = twice(tri(lambda r, c: jnp.where(r < c, 1.0, 0.0)).astype(BF16), 0)
    after = jnp.zeros((1, 1), F32)
    drate = jnp.zeros((1, BLK), F32)
    dkeep = jnp.zeros((1, BLK), F32)
    dskip = jnp.zeros((1, BLK), F32)
    for b in reversed(range(NH)):
        xb, bb, cb = xs[b], bs[b], cs[b]
        xf, bf, cf = xb.astype(F32), bb.astype(F32), cb.astype(F32)
        dy = dv[b]
        a_col, a_row, a_end = chunk_decay(b)
        s_col, s_row = step_col[:, b : b + 1], step[b : b + 1, :]
        later = chain[b] + jnp.exp(after) * leaving
        later_low = later.astype(BF16)
        carried = states[b]
        after = after + a_end
        mix = mixes[b]
        dmix = s_row * dot(halves(dy, 1), twice(xb, 1), NT)
        dgram_low = (fades[b] * dmix).astype(BF16)
        to_end = jnp.exp(jnp.minimum(a_end - a_col, 0.0))
        du = dot(mix.astype(BF16), dy.astype(BF16), TN) + to_end * dot(bb, later_low)
        dx[b] = (s_col * du + skip * dy).astype(BF16)
        dc_far = jnp.exp(a_col) * dot(*thirds(dy, carried, 1), NT)
        db_far = to_end * s_col * dot(twice(xb, 1), halves(later, 1), NT)
        dbc[0, b] = (dot(dgram_low, cb, TN) + db_far).astype(BF16)
        dbc[1, b] = (dot(dgram_low, bb) + dc_far).astype(BF16)
        crossing = dot(halves(mix * dmix, 1), strict)
        far_out = jnp.sum(cf * dc_far, axis=1, keepdims=True)
        far_in = jnp.sum(bf * db_far, axis=1, keepdims=True)
        dlog = jnp.sum(jnp.where(causal, crossing + far_out, far_in), axis=0, keepdims=True)
        dlog = dlog + jnp.exp(a_end) * jnp.sum(later * carried)
        direct = jnp.sum(xf * du, axis=1, keepdims=True)
        direct = jnp.sum(jnp.where(same, direct, 0.0), axis=0, keepdims=True)
        dst[b] = jnp.broadcast_to(direct - rate * dlog, (NH, BLK))
        drate = drate - s_row * dlog
        dkeep = dkeep + starts[b : b + 1, :] * dlog
        dskip = dskip + jnp.sum(dy * xf, axis=0, keepdims=True)

    row = lax.broadcasted_iota(jnp.int32, (NH, BLK), 0)
    lane = lax.broadcasted_iota(jnp.int32, (NH, BLK), 1)
    dkeep = jnp.sum(dkeep, axis=1, keepdims=True) / jnp.full((1, 1), keep, F32)
    drate = jnp.sum(drate, axis=1, keepdims=True)
    dskip = jnp.sum(dskip, axis=1, keepdims=True)
    tile = jnp.where(row == 0, drate, jnp.where(row == 1, dkeep, jnp.where(row == 2, dskip, 0.0)))
    tile = jnp.where(lane == z, tile, 0.0)

    def spread(src, buf, place, axis, peers, sems, rsems):
        copies = []
        for i, peer in enumerate(peers):
            copy = pltpu.make_async_remote_copy(
                src_ref=src, dst_ref=buf.at[place],
                send_sem=sems.at[i], recv_sem=rsems.at[place],
                device_id={axis: peer}, device_id_type=MESH,
            )
            copy.start()
            copies.append(copy)
        return copies

    def gathered(buf, place, count, copies, rsems):
        for o in range(1, count):
            source = lax.rem(place + o, count)
            ref = buf.at[source]
            pltpu.make_async_copy(ref, ref, rsems.at[source]).wait()
        for copy in copies:
            copy.wait_send()

    par_x[at_x] = tile

    def fold(kind, up, slot):
        return pltpu.make_async_remote_copy(
            src_ref=folds.at[kind, up, slot], dst_ref=folds.at[kind, up, slot],
            send_sem=fold_send.at[kind, up, slot], recv_sem=fold_recv.at[kind, up, slot],
            device_id={"seq": lax.rem(me + (2 if up else 2 * NH - 2), 2 * NH)},
            device_id_type=MESH,
        )

    def fold_came(kind, up, slot):
        ref = folds.at[kind, up, slot]
        pltpu.make_async_copy(ref, ref, fold_recv.at[kind, up, slot]).wait()

    def fold_place(dist, up):
        holder = lax.rem(z + (dist if up else NH - dist), NH)
        return holder // (NH // 2) == core, lax.rem(holder, NH // 2)

    def fold_kinds(dist, up):
        return [(kind, reach) for kind, reach in ((0, 4 - up), (1, 3 + up)) if dist <= reach]

    def fold_step(dist):
        for up in (0, 1):
            ours, slot = fold_place(dist, up)

            @pl.when(ours)
            def _():
                for kind, reach in fold_kinds(dist, up):
                    own_part = dbc[kind, pl.ds(2 * slot, 2)]
                    if dist < reach:
                        fold_came(kind, up, slot)
                        total = own_part.astype(F32) + folds[kind, up, slot].astype(F32)
                        folds[kind, up, slot] = total.astype(BF16)
                    else:
                        folds[kind, up, slot] = own_part
                    fold(kind, up, slot).start()

    def send_blocks(kinds, first, count):
        for off in range(first, first + count):
            send_out(kinds, lax.rem(hold_slot + off, NH))

    fold_step(4)
    send_blocks((DX, DST), 0, NH // 2)
    x_copies = spread(par_x.at[at_x], par_x, at_x, "dp", x_peers, x_send, x_recv)
    lax.fori_loop(1, NH - 2, score_grads, 0)
    fold_step(3)
    send_blocks((DX, DST), NH // 2, NH // 2)
    lax.fori_loop(NH - 2, NH, score_grads, 0)
    lax.fori_loop(0, NH, dk_for_partner, 0)
    dk_copy = pair(dk_out, dk_in, 4)
    dk_copy.start()
    gathered(par_x, at_x, nx, x_copies, x_recv)
    par_y[at_y] = jnp.sum(par_x[...], axis=0)
    y_copies = spread(par_y.at[at_y], par_y, at_y, "dp", y_peers, y_send, y_recv)
    fold_step(2)
    lax.fori_loop(0, NH, dk_for_me, 0)
    dk_copy.wait()
    for b in range(NH):
        dqk[b] = (dk[b] + dk_in[b].astype(F32) + dqs[b].astype(F32)).astype(BF16)
    send_blocks((DQK,), 0, NH // 2)
    fold_step(1)
    gathered(par_y, at_y, ny, y_copies, y_recv)
    par_mine[...] = jnp.sum(par_y[...], axis=0)
    own = pltpu.make_async_copy(par_mine, par_z.at[me], z_recv.at[me])
    own.start()
    z_copies = spread(par_mine, par_z, me, "seq", z_peers, z_send, z_recv)
    send_blocks((DQK,), NH // 2, NH // 2)
    last_half = z // (NH // 2) == core
    last_slot = lax.rem(z, NH // 2)
    to_me = pltpu.make_async_copy(whole.at[core], dbc_got, last_recv.at[0])
    to_partner = pltpu.make_async_remote_copy(
        src_ref=whole.at[1 - core], dst_ref=dbc_got, send_sem=last_send.at[0],
        recv_sem=last_recv.at[0], device_id={"seq": partner}, device_id_type=MESH,
    )

    @pl.when(last_half)
    def _():
        for kind in range(2):
            fold_came(kind, 0, last_slot)
            fold_came(kind, 1, last_slot)
            total = dbc[kind, pl.ds(2 * last_slot, 2)].astype(F32)
            total = total + folds[kind, 0, last_slot].astype(F32)
            total = (total + folds[kind, 1, last_slot].astype(F32)).astype(BF16)
            whole[0, kind] = total[0]
            whole[1, kind] = total[1]
        to_partner.start()
        to_me.start()


    for kind in range(6):
        for off in offsets[kind]:
            in_remote(kind, off).wait_send()

    @pl.when(jnp.logical_not(stay))
    def _():
        for kind in range(6):
            in_remote(kind, 0).wait_send()

    for dist, sign, onward in hops:

        @pl.when(from_half(dist, sign))
        def _():
            for j in range(2):
                for kind in onward:
                    hop(kind, dist, sign, j).wait_send()

    for dist in (4, 3, 2, 1):
        for up in (0, 1):
            ours, slot = fold_place(dist, up)

            @pl.when(ours)
            def _():
                for kind, _ in fold_kinds(dist, up):
                    fold(kind, up, slot).wait_send()

    @pl.when(last_half)
    def _():
        to_partner.wait_send()

    pltpu.make_async_copy(dbc_got, dbc_got, last_recv.at[0]).wait()
    outs = (att_got, dqk_got, dx_got, dst_got)
    for c in range(NH):
        for kind in range(4):
            ref = outs[kind].at[0, :, pl.ds(c * BLK, BLK)] if kind in (ATT, DX) else outs[kind].at[c]
            pltpu.make_async_copy(ref, ref, out_recv.at[kind, c]).wait()
    own.wait()
    gathered(par_z, me, 2 * NH, z_copies, z_recv)
    for b in range(NH):

        @pl.when(core * NH + b != me)
        def _():
            for kind in range(4):
                out_remote(kind, b).wait_send()


def epilogue_kernel(
    att_got, dx_got, dqk_got, dbc_got, dst_got, par_z,
    att_out, dq_out, dk_out, dx_out, db_out, dc_out, dstep_out, rate_out, keep_out, skip_out,
):
    att_out[...] = att_got[...]
    dx_out[...] = dx_got[...]
    low = lax.broadcasted_iota(jnp.int32, (BLK, BLK), 1) < 64
    for m in range(NH // 2):
        even, odd = dqk_got[2 * m], dqk_got[2 * m + 1]
        cols = pl.ds(m * BLK, BLK)
        dq_out[0, :, cols] = jnp.where(low, swap_halves(even), odd)
        dk_out[0, :, cols] = jnp.where(low, even, swap_halves(odd))
    for c in range(NH):
        dstep_out[0, c : c + 1, :] = dst_got[c, 0:1, :]
    db_out[0] = dbc_got[0]
    dc_out[0] = dbc_got[1]
    sums = jnp.sum(par_z[...], axis=0)
    rate_out[...] = sums[0:1, 0:NH]
    keep_out[...] = sums[1:2, 0:NH]
    skip_out[...] = sums[2:3, 0:NH]


VM = pl.BlockSpec(memory_space=pltpu.VMEM)
SM = pl.BlockSpec(memory_space=pltpu.SMEM)
ANY = pl.BlockSpec(memory_space=pl.ANY)


def per_device(
    nx, ny, x, b_in, c_out, step, rate, keep, skip, lengths, q, k, lists, go
):
    def arr(*shape, dtype=BF16):
        return jax.ShapeDtypeStruct(shape, dtype)

    def vm(*shape, dtype=BF16):
        return pltpu.VMEM(shape, dtype)

    sq = (BLK, BLK)
    dma = pltpu.SemaphoreType.DMA
    parts = pl.pallas_call(
        partial(main_kernel, nx, ny),
        out_shape=(
            arr(1, BLK, NH * BLK), arr(1, BLK, NH * BLK), arr(NH, *sq), arr(2, *sq),
            arr(NH, NH, BLK, dtype=F32), arr(2 * NH, NH, BLK, dtype=F32),
        ),
        in_specs=[SM] * 5 + [ANY] * 7,
        out_specs=(ANY,) * 6,
        scratch_shapes=[
            vm(BLK, NH * 64), vm(BLK, NH * 64), vm(NH, *sq),
            vm(NH, *sq), vm(NH, *sq), vm(NH, *sq), vm(NH, NH, BLK, dtype=F32),
            vm(2 * NH, *sq), vm(NH, *sq), vm(2 * NH, *sq),
            vm(NH, *sq, dtype=F32), vm(NH, *sq, dtype=F32), vm(NH, *sq, dtype=F32),
            vm(NH, *sq, dtype=F32),
            vm(*sq, dtype=F32), vm(*sq, dtype=F32), vm(NH, *sq), vm(NH, *sq),
            vm(NH, LISTED * BLK, BLK, dtype=F32),
            vm(LISTED * NH, *sq, dtype=F32), vm(LISTED * NH, *sq, dtype=F32),
            vm(NH, *sq, dtype=F32), vm(NH, *sq, dtype=F32), vm(NH, *sq, dtype=F32),
            vm(NH, *sq, dtype=F32), vm(NH, *sq), vm(NH, *sq),
            vm(NH, *sq, dtype=F32), vm(NH, *sq), vm(NH, *sq), vm(2, NH, *sq),
            vm(2, 2, NH // 2, 2, *sq), vm(2, 2, *sq),
            vm(NH, NH, BLK, dtype=F32),
            vm(nx, NH, BLK, dtype=F32), vm(ny, NH, BLK, dtype=F32), vm(NH, BLK, dtype=F32),
            dma((2,)), dma((6, NH)), dma((6, NH)), dma((2, 6, 2)), dma((6,)), dma((6,)), dma((2, NH)), dma((2, NH)),
            dma((2, 2, NH // 2)), dma((2, 2, NH // 2)), dma((1,)), dma((1,)),
            dma((4, NH)), dma((4, NH)),
            dma((nx,)), dma((nx,)), dma((ny,)), dma((ny,)), dma((2 * NH,)), dma((2 * NH,)),
        ],
        compiler_params=pltpu.CompilerParams(collective_id=0, has_side_effects=True),
        name="mixer_attention",
    )(rate, keep, skip, lengths, jnp.transpose(lists, (0, 2, 1)), x, b_in, c_out, step, q, k, go)
    att, dq, dk, dx, db, dc, dstep, drate, dkeep, dskip = pl.pallas_call(
        epilogue_kernel,
        out_shape=(
            arr(1, BLK, NH * BLK), arr(1, BLK, NH * 64), arr(1, BLK, NH * 64),
            arr(1, BLK, NH * BLK), arr(1, *sq), arr(1, *sq), arr(1, NH, BLK, dtype=F32),
            arr(1, NH, dtype=F32), arr(1, NH, dtype=F32), arr(1, NH, dtype=F32),
        ),
        in_specs=[VM] * 6,
        out_specs=(VM,) * 10,
        name="epilogue",
    )(*parts)
    return att, dq, dk, dx, db, dc, dstep, drate.reshape(NH), dkeep.reshape(NH), dskip.reshape(NH)


def solution(mesh):
    rows = P("dp", "seq", None)
    heads = P("dp", None, "seq")
    scene = P("dp", None)
    in_specs = (
        rows, rows, rows, heads, P(), P(), P(), scene, rows, rows, P("dp", None, None), rows,
    )
    out_specs = (rows,) * 6 + (heads, P(), P(), P())
    nx = 4 if mesh.shape["dp"] % 4 == 0 else 1
    ny = mesh.shape["dp"] // nx
    return jax.shard_map(
        partial(per_device, nx, ny), mesh=mesh, in_specs=in_specs, out_specs=out_specs,
        check_vma=False,
    )
```
